256 devices in a mesh: sweep: 4 (over x_lo, core), cross: 64 (over y, z, x_hi).
Axes of the slice: x: 4 (x_hi: 2, x_lo: 2; x = x_hi * 2 + x_lo), y: 4, z: 8, core: 2. Of those that a mesh axis runs over, the one named last changes fastest.
Arguments:
- right_sides: bfloat16 [16, 512, 32, 135], P('sweep', 'cross'), may hold values from -0.099609375 to 0.099609375
- initial: bfloat16 [16, 512, 32, 135], P('sweep', 'cross'), may hold values from -0.099609375 to 0.099609375
- inverse_blocks: bfloat16 [16, 512, 135, 135], P('sweep', 'cross'), may hold values from -0.5 to 0.5
- couplings: bfloat16 [16, 512, 6, 45, 135], P('sweep', 'cross'), may hold values from -0.875 to 0.875
- neighbours: int32 [512, 4], P('cross'), may hold values from 0 to 511, as said below
Outputs:
- result: bfloat16 [16, 512, 32, 135], P('sweep', 'cross')
The draws below stay inside these ranges and needn't reach their ends.
Inputs may be any that keep to these rules, and one draw needn't show every extreme that they name: `neighbours`: columns are numbered device by device along cross, 8 to a device. For a column with local index l on cross device k: face b- names column l of device k - 1 and face b+ column l of device k + 1 (cyclically); face c- names a column of device k - 1 or k, face c+ one of device k or k + 1.
All inputs are finite; a program needn't handle non-finite values.
Results may differ from the reference program's by a relative error of at most 0.029.
Values may be sent and summed in bfloat16 or wider, within the bound.
A program may use at most 64 MiB of HBM per device.

```python
import jax
import jax.numpy as jnp
from jax import lax

NU = 135
NT = 45
R = 32
CC = 8
NPLANES = 16
NCOL = 512


def draw_neighbours(key, part):
    column = jnp.arange(NCOL, dtype=jnp.int32)
    device = column // CC
    key_one, key_two, key_three, key_four = jax.random.split(key, 4)
    face_zero = (column - CC) % NCOL
    face_one = (column + CC) % NCOL
    pick_two = jax.random.randint(key_one, (NCOL,), 0, CC, dtype=jnp.int32)
    step_two = jax.random.randint(key_two, (NCOL,), 0, 2, dtype=jnp.int32)
    pick_three = jax.random.randint(key_three, (NCOL,), 0, CC, dtype=jnp.int32)
    step_three = jax.random.randint(key_four, (NCOL,), 0, 2, dtype=jnp.int32)
    face_two = ((device - step_two) * CC + pick_two) % NCOL
    face_three = ((device + step_three) * CC + pick_three) % NCOL
    return jnp.stack([face_zero, face_one, face_two, face_three], axis=1).astype(jnp.int32)


def levels(stream_key, extent, cuts, smallest, largest):
    factor_of, own = 1.0, jax.random.fold_in(stream_key, 6)
    for dim, blocks in cuts:
        heights = jnp.exp(jax.random.uniform(jax.random.fold_in(own, dim), (blocks,), jnp.float32, smallest / len(cuts), largest / len(cuts)))
        factor_of = factor_of * jnp.repeat(heights, extent[dim] // blocks).reshape([-1 if axis == dim else 1 for axis in range(len(extent))])
    return factor_of


def bell_draw(stream_key, extent, spread, bound, cuts=(), held_as=jnp.bfloat16):
    entries = spread * jax.random.normal(stream_key, extent, jnp.float32)
    if cuts:
        entries = entries * levels(stream_key, extent, cuts, -0.22, 0.18)
    return jnp.clip(entries, -bound, bound).astype(held_as)


def setup_inputs(seed: int = 0) -> dict:
    key_list = jax.random.split(jax.random.key(seed), 6)
    right_sides = jnp.clip(jax.random.uniform(key_list[0], (NPLANES, NCOL, R, NU), jnp.float32, -0.099609375, 0.099609375) * levels(key_list[0], (NPLANES, NCOL, R, NU), ((0, 4), (1, 64)), -0.4, 0.0), -0.099609375, 0.099609375).astype(jnp.bfloat16)
    initial = jnp.clip(jax.random.uniform(key_list[1], (NPLANES, NCOL, R, NU), jnp.float32, -0.099609375, 0.099609375) * levels(key_list[1], (NPLANES, NCOL, R, NU), ((0, 4), (1, 64)), -0.4, 0.0), -0.099609375, 0.099609375).astype(jnp.bfloat16)
    inverse_blocks = bell_draw(key_list[2], (NPLANES, NCOL, NU, NU), (NU * 10 // 9) ** -0.5, 0.5, ((0, 4), (1, 64)))
    couplings = bell_draw(key_list[3], (NPLANES, NCOL, 6, NT, NU), (NT + 5) ** -0.5, 0.875, ((0, 4), (1, 64)))
    neighbours = draw_neighbours(jax.random.fold_in(key_list[5], 71), 0)
    return {"right_sides": right_sides, "initial": initial, "inverse_blocks": inverse_blocks, "couplings": couplings, "neighbours": neighbours}


CROSS_FACES = ((1, 2), (1, 0), (2, 2), (2, 0))


def face_trace(field, axis_place, which):
    lead = field.shape[:-1]
    cube = field.reshape(lead + (5, 3, 3, 3))
    picked = lax.index_in_dim(cube, which, cube.ndim - 3 + axis_place, keepdims=False)
    return picked.reshape(lead + (45,))


def apply_face(coupling, traces):
    return jnp.einsum('cti,crt->cri', coupling.astype(jnp.float32), traces.astype(jnp.float32))


def plane_cross(old_plane, coupling, neighbours):
    total = jnp.zeros(old_plane.shape, jnp.float32)
    for face, (axis_place, which) in enumerate(CROSS_FACES):
        beside = old_plane[neighbours[:, face]]
        total = total + apply_face(coupling[:, 2 + face], face_trace(beside, axis_place, which))
    return total


def solve_plane(inverse, total):
    residue = total.astype(jnp.bfloat16)
    solved = jnp.einsum('cij,crj->cri', inverse.astype(jnp.float32), residue.astype(jnp.float32))
    return solved.astype(jnp.bfloat16)


def reference(right_sides, initial, inverse_blocks, couplings, neighbours):
    zero_plane = jnp.zeros_like(initial[0])
    upper_source = jnp.concatenate([initial[1:], zero_plane[None]], 0)

    def forward(previous, inputs):
        rhs_plane, inverse, coupling, old_plane, upper_plane = inputs
        total = rhs_plane.astype(jnp.float32) - plane_cross(old_plane, coupling, neighbours)
        total = total - apply_face(coupling[:, 1], face_trace(upper_plane, 0, 0))
        total = total - apply_face(coupling[:, 0], face_trace(previous, 0, 2))
        solved = solve_plane(inverse, total)
        return solved, solved

    _unused, middle = lax.scan(forward, zero_plane, (right_sides, inverse_blocks, couplings, initial, upper_source))
    lower_source = jnp.concatenate([zero_plane[None], middle[:-1]], 0)

    def backward(following, inputs):
        rhs_plane, inverse, coupling, mid_plane, lower_plane = inputs
        total = rhs_plane.astype(jnp.float32) - plane_cross(mid_plane, coupling, neighbours)
        total = total - apply_face(coupling[:, 0], face_trace(lower_plane, 0, 2))
        total = total - apply_face(coupling[:, 1], face_trace(following, 0, 0))
        solved = solve_plane(inverse, total)
        return solved, solved

    _unused, result = lax.scan(backward, zero_plane, (right_sides, inverse_blocks, couplings, middle, lower_source), reverse=True)
    return result
```

```python
import functools

import jax
import jax.numpy as jnp
import numpy as np
from jax import lax
from jax.experimental import pallas as pl
from jax.experimental.pallas import tpu as pltpu
from jax.sharding import PartitionSpec as P

MESH = pl.DeviceIdType.MESH
NU, NT, R, CC, NP = 135, 45, 32, 8, 4
FT = 48
LANES = NP * R
F32, BF16 = jnp.float32, jnp.bfloat16
FACES = ((1, 2), (2, 2), (1, 0), (2, 0), (0, 0), (0, 2))
STACK = (1, 2, 3, 4, 5)
NSTACK = len(STACK) * FT
LOWER = 256


def selector():
    rows = np.zeros((len(FACES) * FT, NU), np.float32)
    for face, (axis_place, which) in enumerate(FACES):
        for slot in range(NT):
            v, first, second = slot // 9, slot // 3 % 3, slot % 3
            node = [first, second]
            node.insert(axis_place, which)
            rows[face * FT + slot, v * 27 + node[0] * 9 + node[1] * 3 + node[2]] = 1.0
    return rows


def nn(a, b):
    return lax.dot_general(a, b, (((1,), (0,)), ((), ())), preferred_element_type=F32)


def nt(a, b):
    return lax.dot_general(a, b, (((1,), (1,)), ((), ())), preferred_element_type=F32)


def blocks(rows):
    return lax.broadcasted_iota(jnp.int32, (rows, LANES), 1) // R


def by_block(rows, parts):
    block = blocks(rows)
    total = jnp.zeros((rows, LANES), F32)
    for b, part in parts:
        total = jnp.where(block == b, part, total)
    return total


def kernel(
    crosses,
    neigh,
    sel,
    rhs_hbm,
    init_hbm,
    inv_hbm,
    cpl_hbm,
    out_hbm,
    init_v,
    rhs_v,
    inv_v,
    cpl_v,
    out_v,
    stack_v,
    d_v,
    w_v,
    x_v,
    v_v,
    m_v,
    u_v,
    us_v,
    q_v,
    e_v,
    ext_l0,
    ext_l1,
    ext_r0,
    ext_r1,
    up_s,
    up_r,
    a_s,
    a_r,
    m_s,
    m_r,
    load_sem,
    col_sem,
    out_sem,
    halo_s,
    halo_r,
    upsem,
    a_ss,
    a_rs,
    m_ss,
    m_rs,
):
    ext_l, ext_r = (ext_l0, ext_l1), (ext_r0, ext_r1)
    s = lax.axis_index("sweep")
    k = lax.axis_index("cross")
    right = lax.rem(k + 1, crosses)
    left = lax.rem(k + crosses - 1, crosses)

    load_init = pltpu.make_async_copy(init_hbm, init_v, load_sem.at[0])
    load_rhs = pltpu.make_async_copy(rhs_hbm, rhs_v, load_sem.at[1])
    load_init.start()
    load_rhs.start()

    def inv_load(c):
        return pltpu.make_async_copy(inv_hbm.at[:, c], inv_v.at[:, c], col_sem.at[0, c])

    def cpl_load(c):
        return pltpu.make_async_copy(cpl_hbm.at[:, c], cpl_v.at[:, c], col_sem.at[1, c])

    for c in range(CC):
        inv_load(c).start()
        cpl_load(c).start()

    barrier = pltpu.get_barrier_semaphore()
    for other in (left, right):
        pl.semaphore_signal(barrier, inc=1, device_id={"cross": other}, device_id_type=MESH)
    for step in (1, 2, 3):
        pl.semaphore_signal(
            barrier, inc=1, device_id={"sweep": lax.rem(s + step, 4)}, device_id_type=MESH
        )

    stack_v[...] = jnp.zeros_like(stack_v)
    u_v[...] = jnp.zeros_like(u_v)

    @pl.when(s == 3)
    def _():
        up_r[...] = jnp.zeros_like(up_r)

    for step in (1, 2, 3):

        @pl.when(s < step)
        def _():
            a_r[0, step - 1] = jnp.zeros((FT, CC * R), BF16)

        @pl.when(s + step > 3)
        def _():
            a_r[1, step - 1] = jnp.zeros((FT, CC * R), BF16)

    for step in (1, 2):

        @pl.when(s < step + 1)
        def _():
            m_r[0, step - 1] = jnp.zeros((CC, FT, FT), BF16)

        @pl.when(s + step > 2)
        def _():
            m_r[1, step - 1] = jnp.zeros((CC, FT, FT), BF16)

    load_init.wait()
    up_s[...] = nt(sel[4 * FT : 5 * FT], init_v[0].reshape(CC * R, NU)).astype(BF16)

    def first_traces(g, carry):
        for b in range(4):
            c = 4 * g + b
            picked = nt(sel[0 : 5 * FT], init_v[:, c].reshape(LANES, NU))
            ext_l[0][CC + c] = picked[0 : 2 * FT].astype(BF16)
            ext_r[0][c] = picked[2 * FT : 4 * FT].astype(BF16)
            us_v[c] = pltpu.roll(picked[4 * FT : 5 * FT], LANES - R, 1)
        return carry

    lax.fori_loop(0, 2, first_traces, 0)
    pl.semaphore_wait(barrier, 5)

    def halo(sweep):
        return (
            pltpu.make_async_remote_copy(
                ext_l[sweep].at[pl.ds(CC, CC)],
                ext_l[sweep].at[pl.ds(0, CC)],
                halo_s.at[sweep, 0],
                halo_r.at[sweep, 0],
                device_id={"cross": right},
                device_id_type=MESH,
            ),
            pltpu.make_async_remote_copy(
                ext_r[sweep].at[pl.ds(0, CC)],
                ext_r[sweep].at[pl.ds(CC, CC)],
                halo_s.at[sweep, 1],
                halo_r.at[sweep, 1],
                device_id={"cross": left},
                device_id_type=MESH,
            ),
        )

    up_copy = pltpu.make_async_remote_copy(
        up_s,
        up_r,
        upsem.at[0],
        upsem.at[1],
        device_id={"sweep": lax.rem(s + 3, 4)},
        device_id_type=MESH,
    )
    for copy in halo(0):
        copy.start()

    @pl.when(s > 0)
    def _():
        up_copy.start()

    def a_copy(sweep, step):
        to = lax.rem(s + step, 4) if sweep == 0 else lax.rem(s + 4 - step, 4)
        return pltpu.make_async_remote_copy(
            a_s.at[sweep],
            a_r.at[sweep, step - 1],
            a_ss.at[sweep, step - 1],
            a_rs.at[sweep, step - 1],
            device_id={"sweep": to},
            device_id_type=MESH,
        )

    def m_copy(sweep, step):
        to = lax.rem(s + step, 4) if sweep == 0 else lax.rem(s + 4 - step, 4)
        return pltpu.make_async_remote_copy(
            m_s.at[sweep],
            m_r.at[sweep, step - 1],
            m_ss.at[sweep, step - 1],
            m_rs.at[sweep, step - 1],
            device_id={"sweep": to},
            device_id_type=MESH,
        )

    def a_sends(sweep, step):
        return s + step < 4 if sweep == 0 else s >= step

    def a_takes(sweep, step):
        return s >= step if sweep == 0 else s + step < 4

    def m_sends(sweep, step):
        if sweep == 0:
            return jnp.logical_and(s >= 1, s + step < 4)
        return jnp.logical_and(s <= 2, s >= step)

    def m_takes(sweep, step):
        return s >= step + 1 if sweep == 0 else s + step <= 2

    load_rhs.wait()

    def products(g, carry):
        for b in range(4):
            c = 4 * g + b
            inv_load(c).wait()
            cpl_load(c).wait()
            for p in range(NP):
                for place, face in enumerate(STACK):
                    stack_v[p, FT * place : FT * place + NT] = cpl_v[p, c, face]
                stack_v[p, LOWER : LOWER + NT] = cpl_v[p, c, 0]
                d_v[p, c] = nt(inv_v[p, c], stack_v[p]).astype(BF16)
            rhs = rhs_v[:, c].reshape(LANES, NU)
            w_v[c] = by_block(NU, [(p, nt(inv_v[p, c], rhs)) for p in range(NP)])
        return carry

    lax.fori_loop(0, 2, products, 0)

    def d_in(sweep, p, c):
        if sweep == 0:
            return d_v[p, c, :, LOWER : LOWER + FT]
        return d_v[p, c, :, 0:FT]

    def sections(sweep):
        order = range(NP) if sweep == 0 else range(NP - 1, -1, -1)
        rows = sel[5 * FT : 6 * FT] if sweep == 0 else sel[4 * FT : 5 * FT]

        def body(g, carry):
            for b in range(4):
                c = 4 * g + b
                before = None
                for p in order:
                    d = d_in(sweep, p, c)
                    q = nn(rows, d).astype(BF16)
                    q_v[sweep, c, p] = q
                    if before is None:
                        e_v[sweep, c, p] = d
                        before = -q
                    else:
                        e_v[sweep, c, p] = nn(d, before).astype(BF16)
                        before = (-nn(q, before)).astype(BF16)
                m_s[sweep, c] = before
            return carry

        lax.fori_loop(0, 2, body, 0)
        for step in (1, 2):

            @pl.when(m_sends(sweep, step))
            def _():
                m_copy(sweep, step).start()

    sections(0)

    def gathered(sweep, c, upper):
        low = lax.rem(neigh[c, 2] - (k - 1) * CC + 2 * crosses * CC, crosses * CC)
        high = lax.rem(neigh[c, 3] - k * CC + crosses * CC, crosses * CC)
        low = jnp.clip(low, 0, 2 * CC - 1)
        high = jnp.clip(high, 0, 2 * CC - 1)
        return jnp.concatenate(
            [
                upper,
                ext_l[sweep][c, 0:FT],
                ext_r[sweep][CC + c, 0:FT],
                ext_l[sweep][low, FT : 2 * FT],
                ext_r[sweep][high, FT : 2 * FT],
            ],
            axis=0,
        )

    def local_sweep(sweep, c, base, upper):
        order = list(range(NP)) if sweep == 0 else list(range(NP - 1, -1, -1))
        shift = R if sweep == 0 else LANES - R
        stack = gathered(sweep, c, upper)
        x = by_block(NU, [(p, nn(d_v[p, c, :, 0:NSTACK], stack)) for p in range(NP)])
        v = base - x
        v_v[c] = v
        if sweep == 0:
            x_v[c] = x
        start = 18 if sweep == 0 else 0
        for var in range(5):
            u_v[c, 9 * var : 9 * var + 9] = v_v[c, 27 * var + start : 27 * var + start + 9]
        u = u_v[c]
        block = blocks(FT)
        now = u
        for p in order[1:]:
            z = nn(q_v[sweep, c, p], pltpu.roll(now, shift, 1).astype(BF16))
            now = jnp.where(block == p, u - z, now)
        before = jnp.where(block == order[0], 0.0, pltpu.roll(now, shift, 1)).astype(BF16)
        y = by_block(NU, [(p, nn(d_in(sweep, p, c), before)) for p in order[1:]])
        m_v[c] = v - y
        return now

    def packed(sweep, c, b, now, total):
        last = 3 if sweep == 0 else 0
        turned = now if b == last else pltpu.roll(now, (R * (b - last)) % LANES, 1)
        return jnp.where(blocks(FT) == b, turned, total)

    def spread(b, group):
        one = jnp.where(blocks(FT) == b, group, 0.0)
        one = one + pltpu.roll(one, R, 1)
        return (one + pltpu.roll(one, 2 * R, 1)).astype(BF16)

    def send_ends(sweep):
        for step in (1, 2, 3):

            @pl.when(a_sends(sweep, step))
            def _():
                a_copy(sweep, step).start()

    def take_ends(sweep):
        for step in (1, 2, 3):

            @pl.when(a_takes(sweep, step))
            def _():
                a_copy(sweep, step).wait_recv()

        for step in (1, 2):

            @pl.when(m_takes(sweep, step))
            def _():
                m_copy(sweep, step).wait_recv()

    def incoming(sweep, g):
        lanes = slice(LANES * g, LANES * g + LANES)
        far = a_r[sweep, 2, :, lanes]
        mid = a_r[sweep, 1, :, lanes].astype(F32) + by_block(
            FT, [(b, nn(m_r[sweep, 1, 4 * g + b], far)) for b in range(4)]
        )
        mid = mid.astype(BF16)
        return a_r[sweep, 0, :, lanes].astype(F32) + by_block(
            FT, [(b, nn(m_r[sweep, 0, 4 * g + b], mid)) for b in range(4)]
        )

    def corrected(sweep, c, b, entering):
        t = spread(b, entering)
        return m_v[c] - by_block(NU, [(p, nn(e_v[sweep, c, p], t)) for p in range(NP)])

    for copy in halo(0):
        copy.wait_recv()

    @pl.when(s < 3)
    def _():
        up_copy.wait_recv()

    for g in range(2):
        total = jnp.zeros((FT, LANES), F32)
        for b in range(4):
            c = 4 * g + b
            edge = up_r[:, LANES * g : LANES * g + LANES].astype(F32)
            edge = pltpu.roll(edge, (R * (3 - b)) % LANES, 1) if b != 3 else edge
            upper = jnp.where(blocks(FT) == 3, edge, us_v[c]).astype(BF16)
            total = packed(0, c, b, local_sweep(0, c, w_v[c], upper), total)
        a_s[0, :, LANES * g : LANES * g + LANES] = total.astype(BF16)
    send_ends(0)
    take_ends(0)
    for g in range(2):
        entering = incoming(0, g)
        for b in range(4):
            c = 4 * g + b
            middle = corrected(0, c, b, entering)
            picked = nn(sel[0 : 4 * FT], middle.astype(BF16)).astype(BF16)
            ext_l[1][CC + c] = picked[0 : 2 * FT]
            ext_r[1][c] = picked[2 * FT : 4 * FT]
            w_v[c] = middle + x_v[c]
    for copy in halo(1):
        copy.start()
    sections(1)

    for copy in halo(1):
        copy.wait_recv()
    nothing = jnp.zeros((FT, LANES), BF16)
    for g in range(2):
        total = jnp.zeros((FT, LANES), F32)
        for b in range(4):
            c = 4 * g + b
            total = packed(1, c, b, local_sweep(1, c, w_v[c], nothing), total)
        a_s[1, :, LANES * g : LANES * g + LANES] = total.astype(BF16)
    send_ends(1)
    take_ends(1)
    same = (
        lax.broadcasted_iota(jnp.int32, (LANES, LANES), 0)
        == lax.broadcasted_iota(jnp.int32, (LANES, LANES), 1)
    ).astype(BF16)

    def out_store(c):
        return pltpu.make_async_copy(out_v.at[:, c], out_hbm.at[:, c], out_sem.at[c])

    for g in range(2):
        entering = incoming(1, g)
        for b in range(4):
            c = 4 * g + b
            result = corrected(1, c, b, entering).astype(BF16)
            out_v[:, c] = nt(same, result).astype(BF16).reshape(NP, R, NU)
            out_store(c).start()
    for c in range(CC):
        out_store(c).wait()

    for sweep in (0, 1):
        for copy in halo(sweep):
            copy.wait_send()
        for step in (1, 2, 3):

            @pl.when(a_sends(sweep, step))
            def _():
                a_copy(sweep, step).wait_send()

        for step in (1, 2):

            @pl.when(m_sends(sweep, step))
            def _():
                m_copy(sweep, step).wait_send()

    @pl.when(s > 0)
    def _():
        up_copy.wait_send()


def local(crosses, right_sides, initial, inverse_blocks, couplings, neighbours):
    anywhere = pl.BlockSpec(memory_space=pl.ANY)
    vmem = pltpu.VMEM
    dma = pltpu.SemaphoreType.DMA
    return pl.pallas_call(
        functools.partial(kernel, crosses),
        out_shape=jax.ShapeDtypeStruct(right_sides.shape, BF16),
        in_specs=[
            pl.BlockSpec(memory_space=pltpu.SMEM),
            pl.BlockSpec(memory_space=pltpu.VMEM),
            anywhere,
            anywhere,
            anywhere,
            anywhere,
        ],
        out_specs=anywhere,
        scratch_shapes=[
            vmem((NP, CC, R, NU), BF16),
            vmem((NP, CC, R, NU), BF16),
            vmem((NP, CC, NU, NU), BF16),
            vmem((NP, CC, 6, NT, NU), BF16),
            vmem((NP, CC, R, NU), BF16),
            vmem((NP, LOWER + FT, NU), BF16),
            vmem((NP, CC, NU, LOWER + FT), BF16),
            vmem((CC, NU, LANES), F32),
            vmem((CC, NU, LANES), F32),
            vmem((CC, NU, LANES), F32),
            vmem((CC, NU, LANES), F32),
            vmem((CC, FT, LANES), F32),
            vmem((CC, FT, LANES), F32),
            vmem((2, CC, NP, FT, FT), BF16),
            vmem((2, CC, NP, NU, FT), BF16),
            vmem((2 * CC, 2 * FT, LANES), BF16),
            vmem((2 * CC, 2 * FT, LANES), BF16),
            vmem((2 * CC, 2 * FT, LANES), BF16),
            vmem((2 * CC, 2 * FT, LANES), BF16),
            vmem((FT, CC * R), BF16),
            vmem((FT, CC * R), BF16),
            vmem((2, FT, CC * R), BF16),
            vmem((2, 3, FT, CC * R), BF16),
            vmem((2, CC, FT, FT), BF16),
            vmem((2, 2, CC, FT, FT), BF16),
            dma((2,)),
            dma((2, CC)),
            dma((CC,)),
            dma((2, 2)),
            dma((2, 2)),
            dma((2,)),
            dma((2, 3)),
            dma((2, 3)),
            dma((2, 2)),
            dma((2, 2)),
        ],
        compiler_params=pltpu.CompilerParams(
            collective_id=0, has_side_effects=True, vmem_limit_bytes=50 * 1024 * 1024
        ),
        name="sweeps",
    )(
        neighbours,
        jnp.asarray(selector(), BF16),
        right_sides,
        initial,
        inverse_blocks,
        couplings,
    )


def solution(mesh):
    return jax.shard_map(
        functools.partial(local, mesh.shape["cross"]),
        mesh=mesh,
        in_specs=(
            P("sweep", "cross", None, None),
            P("sweep", "cross", None, None),
            P("sweep", "cross", None, None),
            P("sweep", "cross", None, None, None),
            P("cross", None),
        ),
        out_specs=P("sweep", "cross", None, None),
        check_vma=False,
    )
```

```python
import functools

import jax
import jax.numpy as jnp
import numpy as np
from jax import lax
from jax.experimental import pallas as pl
from jax.experimental.pallas import tpu as pltpu
from jax.sharding import PartitionSpec as P

MESH = pl.DeviceIdType.MESH
NU, NT, R, CC, NP = 135, 45, 32, 8, 4
FT = 48
LANES = NP * R
NUP = 144
F32, BF16 = jnp.float32, jnp.bfloat16
FACES = ((1, 2), (2, 2), (1, 0), (2, 0), (0, 0), (0, 2))
STACK = (1, 2, 3, 4, 5)
NSTACK = len(STACK) * FT
LOWER = 256


def selector():
    rows = np.zeros((len(FACES) * FT, NU), np.float32)
    for face, (axis_place, which) in enumerate(FACES):
        for slot in range(NT):
            v, first, second = slot // 9, slot // 3 % 3, slot % 3
            node = [first, second]
            node.insert(axis_place, which)
            rows[face * FT + slot, v * 27 + node[0] * 9 + node[1] * 3 + node[2]] = 1.0
    return rows


def nn(a, b):
    return lax.dot_general(a, b, (((1,), (0,)), ((), ())), preferred_element_type=F32)


def nt(a, b):
    return lax.dot_general(a, b, (((1,), (1,)), ((), ())), preferred_element_type=F32)


def blocks(rows):
    return lax.broadcasted_iota(jnp.int32, (rows, LANES), 1) // R


def by_block(rows, parts):
    block = blocks(rows)
    total = parts[0][1]
    for b, part in parts[1:]:
        total = jnp.where(block == b, part, total)
    return total


def kernel(
    crosses,
    neigh,
    sel,
    rhs_hbm,
    init_hbm,
    inv_hbm,
    cpl_hbm,
    out_v,
    init_v,
    rhs_v,
    inv_n,
    cpl_n,
    turn_v,
    inv_v,
    stack_v,
    d_v,
    rows_v,
    w_v,
    x_v,
    v_v,
    t_v,
    us_v,
    q_v,
    l1_v,
    l2_v,
    l3_v,
    li_v,
    ext_l0,
    ext_l1,
    ext_r0,
    ext_r1,
    up_s,
    up_r,
    a_s,
    a_r,
    m_s,
    m_r,
    load_sem,
    plane_sem,
    halo_s,
    halo_r,
    upsem,
    a_ss,
    a_rs,
    m_ss,
    m_rs,
):
    ext_l, ext_r = (ext_l0, ext_l1), (ext_r0, ext_r1)
    s = lax.axis_index("sweep")
    k = lax.axis_index("cross")
    right = lax.rem(k + 1, crosses)
    left = lax.rem(k + crosses - 1, crosses)

    load_init = pltpu.make_async_copy(init_hbm, init_v, load_sem.at[0])
    load_rhs = pltpu.make_async_copy(rhs_hbm, rhs_v, load_sem.at[1])

    def inv_load(p):
        return pltpu.make_async_copy(inv_hbm.at[p], inv_n.at[p], plane_sem.at[0, p])

    def cpl_load(p):
        return pltpu.make_async_copy(cpl_hbm.at[p], cpl_n.at[p], plane_sem.at[1, p])

    load_init.start()
    for p in range(NP):
        inv_load(p).start()
        cpl_load(p).start()
    load_rhs.start()

    barrier = pltpu.get_barrier_semaphore()
    for other in (left, right):
        pl.semaphore_signal(barrier, inc=1, device_id={"cross": other}, device_id_type=MESH)
    for step in (1, 2, 3):
        pl.semaphore_signal(
            barrier, inc=1, device_id={"sweep": lax.rem(s + step, 4)}, device_id_type=MESH
        )

    load_init.wait()
    up_s[...] = nt(sel[4 * FT : 5 * FT], init_v[0].reshape(CC * R, NU)).astype(BF16)
    for c in range(CC):
        picked = nt(sel[0 : 5 * FT], init_v[:, c].reshape(LANES, NU))
        ext_l[0][CC + c] = picked[0 : 2 * FT].astype(BF16)
        ext_r[0][c] = picked[2 * FT : 4 * FT].astype(BF16)
        us_v[c] = pltpu.roll(picked[4 * FT : 5 * FT], LANES - R, 1)
    pl.semaphore_wait(barrier, 5)

    def halo(sweep):
        return (
            pltpu.make_async_remote_copy(
                ext_l[sweep].at[pl.ds(CC, CC)],
                ext_l[sweep].at[pl.ds(0, CC)],
                halo_s.at[sweep, 0],
                halo_r.at[sweep, 0],
                device_id={"cross": right},
                device_id_type=MESH,
            ),
            pltpu.make_async_remote_copy(
                ext_r[sweep].at[pl.ds(0, CC)],
                ext_r[sweep].at[pl.ds(CC, CC)],
                halo_s.at[sweep, 1],
                halo_r.at[sweep, 1],
                device_id={"cross": left},
                device_id_type=MESH,
            ),
        )

    up_copy = pltpu.make_async_remote_copy(
        up_s,
        up_r,
        upsem.at[0],
        upsem.at[1],
        device_id={"sweep": lax.rem(s + 3, 4)},
        device_id_type=MESH,
    )
    for copy in halo(0):
        copy.start()

    @pl.when(s > 0)
    def _():
        up_copy.start()

    def a_copy(sweep, step):
        to = lax.rem(s + step, 4) if sweep == 0 else lax.rem(s + 4 - step, 4)
        return pltpu.make_async_remote_copy(
            a_s.at[sweep],
            a_r.at[sweep, step - 1],
            a_ss.at[sweep, step - 1],
            a_rs.at[sweep, step - 1],
            device_id={"sweep": to},
            device_id_type=MESH,
        )

    def m_copy(sweep, step):
        to = lax.rem(s + step, 4) if sweep == 0 else lax.rem(s + 4 - step, 4)
        return pltpu.make_async_remote_copy(
            m_s.at[sweep],
            m_r.at[sweep, step - 1],
            m_ss.at[sweep, step - 1],
            m_rs.at[sweep, step - 1],
            device_id={"sweep": to},
            device_id_type=MESH,
        )

    def a_sends(sweep, step):
        return s + step < 4 if sweep == 0 else s >= step

    def a_takes(sweep, step):
        return s >= step if sweep == 0 else s + step < 4

    def m_sends(sweep, step):
        if sweep == 0:
            return jnp.logical_and(s >= 1, s + step < 4)
        return jnp.logical_and(s <= 2, s >= step)

    def m_takes(sweep, step):
        return s >= step + 1 if sweep == 0 else s + step <= 2

    @pl.when(s == 3)
    def _():
        up_r[...] = jnp.zeros_like(up_r)

    for step in (1, 2, 3):

        @pl.when(s < step)
        def _():
            a_r[0, step - 1] = jnp.zeros((FT, CC * R), BF16)

        @pl.when(s + step > 3)
        def _():
            a_r[1, step - 1] = jnp.zeros((FT, CC * R), BF16)

    for step in (1, 2):

        @pl.when(s < step + 1)
        def _():
            m_r[0, step - 1] = jnp.zeros((CC, FT, FT), BF16)

        @pl.when(s + step > 2)
        def _():
            m_r[1, step - 1] = jnp.zeros((CC, FT, FT), BF16)

    inv_v[:, :, NU - 7 : NUP] = jnp.zeros((CC, NP, NUP - NU + 7, NU), BF16)
    for place in list(range(len(STACK))) + [LOWER // FT]:
        top = LOWER if place == LOWER // FT else FT * place
        stack_v[:, :, top + 32 : top + FT] = jnp.zeros((CC, NP, 16, NU), BF16)
    stack_v[:, :, NSTACK:LOWER] = jnp.zeros((CC, NP, LOWER - NSTACK, NU), BF16)
    q_v[...] = jnp.zeros_like(q_v)

    def turn(slot, block, count, to, p, first):
        flat = block.astype(F32).reshape(CC * count, NU)
        turn_v[0, slot, 0 : CC * count] = flat[:, 0:128]
        turn_v[1, slot, 0 : CC * count, 0 : NU - 128] = flat[:, 128:NU]
        for c in range(CC):
            rows = pl.ds(c, count, stride=CC)
            to[c, p, first : first + count, 0:128] = turn_v[0, slot, rows].astype(BF16)
            to[c, p, first : first + count, 128:NU] = turn_v[1, slot, rows][
                :, 0 : NU - 128
            ].astype(BF16)

    def products(p, carry):
        inv_load(p).wait()
        cpl_load(p).wait()
        slot = 0
        for first in range(0, NU, 16):
            count = min(16, NU - first)
            turn(slot, inv_n[p, first : first + count], count, inv_v, p, first)
            slot += 1
        for top, face in [(FT * place, face) for place, face in enumerate(STACK)] + [(LOWER, 0)]:
            for first in range(0, NT, 16):
                count = min(16, NT - first)
                block = cpl_n[p, face, first : first + count]
                turn(slot, block, count, stack_v, p, top + first)
                slot += 1
        for c in range(CC):
            d = nt(inv_v[c, p], stack_v[c, p])
            d_v[c, p] = d.astype(BF16)
            rows_v[0, c] = d[:, LOWER : LOWER + FT]
            rows_v[1, c] = d[:, 0:FT]
            for var in range(5):
                to = slice(9 * var, 9 * var + 9)
                q_v[0, c, p, to] = rows_v[0, c, 27 * var + 18 : 27 * var + 27]
                q_v[1, c, p, to] = rows_v[1, c, 27 * var : 27 * var + 9]
        return carry

    lax.fori_loop(0, NP, products, 0)
    load_rhs.wait()

    def by_plane(rows, stacked):
        return by_block(rows, [(p, stacked[rows * p : rows * p + rows]) for p in range(NP)])

    for c in range(CC):
        rhs = rhs_v[:, c].reshape(LANES, NU)
        w_v[c] = by_plane(NUP, nt(inv_v[c].reshape(NP * NUP, NU), rhs))

    def order_of(sweep):
        return list(range(NP)) if sweep == 0 else list(range(NP - 1, -1, -1))

    def sections(sweep):
        order = order_of(sweep)
        n = [[(-q_v[sweep, c, p]).astype(BF16) for p in order] for c in range(CC)]
        two = [
            [nn(n[c][o], n[c][o - 1]).astype(BF16) for o in (1, 2, 3)] for c in range(CC)
        ]
        for c in range(CC):
            for o in (1, 2, 3):
                l1_v[sweep, c, FT * (o - 1) : FT * o] = n[c][o]
            for o in (2, 3):
                l2_v[sweep, c, FT * (o - 2) : FT * (o - 1)] = two[c][o - 1]
            li_v[sweep, c, 0:FT] = n[c][0]
            li_v[sweep, c, FT : 2 * FT] = two[c][0]
            li_v[sweep, c, 2 * FT : 3 * FT] = nn(two[c][1], n[c][0]).astype(BF16)
            l3_v[sweep, c] = nn(two[c][2], n[c][1]).astype(BF16)
            m_s[sweep, c] = nn(two[c][2], two[c][0]).astype(BF16)
        for step in (1, 2):

            @pl.when(m_sends(sweep, step))
            def _():
                m_copy(sweep, step).start()

    sections(0)

    def gathered(sweep, c, upper):
        low = lax.rem(neigh[2, c] - (k - 1) * CC + 2 * crosses * CC, crosses * CC)
        high = lax.rem(neigh[3, c] - k * CC + crosses * CC, crosses * CC)
        low = jnp.clip(low, 0, 2 * CC - 1)
        high = jnp.clip(high, 0, 2 * CC - 1)
        return jnp.concatenate(
            [
                upper,
                ext_l[sweep][c, 0:FT],
                ext_r[sweep][CC + c, 0:FT],
                ext_l[sweep][low, FT : 2 * FT],
                ext_r[sweep][high, FT : 2 * FT],
            ],
            axis=0,
        )

    def shift_of(sweep, steps):
        return R * steps if sweep == 0 else LANES - R * steps

    def local_sweep(sweep, c, base, upper):
        order = order_of(sweep)
        stack = gathered(sweep, c, upper)
        x = by_plane(NUP, nn(d_v[c].reshape(NP * NUP, LOWER + FT)[:, 0:NSTACK], stack))
        v = base - x
        v_v[c] = v
        if sweep == 0:
            x_v[c] = x
        start = 18 if sweep == 0 else 0
        pieces = [v_v[c, 27 * var + start : 27 * var + start + 9] for var in range(5)]
        for var in range(5):
            t_v[c, 9 * var : 9 * var + 9] = pieces[var]
        u = t_v[c]
        block = blocks(FT)
        total = u
        for steps, left_v in ((1, l1_v), (2, l2_v), (3, l3_v)):
            moved = pltpu.roll(u, shift_of(sweep, steps), 1).astype(BF16)
            z = nn(left_v[sweep, c], moved)
            for o in range(steps, NP):
                part = z[FT * (o - steps) : FT * (o - steps + 1)]
                total = total + jnp.where(block == order[o], part, 0.0)
        return total

    def packed(sweep, b, now, total):
        last = 3 if sweep == 0 else 0
        turned_in = now if b == last else pltpu.roll(now, (R * (b - last)) % LANES, 1)
        return jnp.where(blocks(FT) == b, turned_in, total)

    def spread(b, group):
        one = jnp.where(blocks(FT) == b, group, 0.0)
        one = one + pltpu.roll(one, R, 1)
        return one + pltpu.roll(one, 2 * R, 1)

    def send_ends(sweep):
        for step in (1, 2, 3):

            @pl.when(a_sends(sweep, step))
            def _():
                a_copy(sweep, step).start()

    def take_ends(sweep):
        for step in (1, 2, 3):

            @pl.when(a_takes(sweep, step))
            def _():
                a_copy(sweep, step).wait_recv()

        for step in (1, 2):

            @pl.when(m_takes(sweep, step))
            def _():
                m_copy(sweep, step).wait_recv()

    def incoming(sweep, g):
        lanes = slice(LANES * g, LANES * g + LANES)

        def applied(step, ends):
            return by_block(FT, [(b, nn(m_r[sweep, step, 4 * g + b], ends)) for b in range(4)])

        mid = a_r[sweep, 1, :, lanes].astype(F32) + applied(1, a_r[sweep, 2, :, lanes])
        return a_r[sweep, 0, :, lanes].astype(F32) + applied(0, mid.astype(BF16))

    def corrected(sweep, c, b, entering):
        order = order_of(sweep)
        t = spread(b, entering)
        z = nn(li_v[sweep, c], t.astype(BF16))
        before = by_block(
            FT, [(order[0], t)] + [(order[o], z[FT * (o - 1) : FT * o]) for o in (1, 2, 3)]
        )
        local_part = pltpu.roll(t_v[c], shift_of(sweep, 1), 1)
        before = before + jnp.where(blocks(FT) == order[0], 0.0, local_part)
        low = LOWER if sweep == 0 else 0
        d = d_v[c].reshape(NP * NUP, LOWER + FT)[:, low : low + FT]
        return v_v[c] - by_plane(NUP, nn(d, before.astype(BF16)))

    for copy in halo(0):
        copy.wait_recv()

    @pl.when(s < 3)
    def _():
        up_copy.wait_recv()

    t_v[...] = jnp.zeros_like(t_v)
    for g in range(2):
        total = jnp.zeros((FT, LANES), F32)
        for b in range(4):
            c = 4 * g + b
            edge = up_r[:, LANES * g : LANES * g + LANES].astype(F32)
            edge = pltpu.roll(edge, (R * (3 - b)) % LANES, 1) if b != 3 else edge
            upper = jnp.where(blocks(FT) == 3, edge, us_v[c]).astype(BF16)
            now = local_sweep(0, c, w_v[c], upper)
            t_v[c] = now
            total = packed(0, b, now, total)
        a_s[0, :, LANES * g : LANES * g + LANES] = total.astype(BF16)
    send_ends(0)
    take_ends(0)
    for g in range(2):
        entering = incoming(0, g)
        for b in range(4):
            c = 4 * g + b
            middle = corrected(0, c, b, entering)
            picked = nn(sel[0 : 4 * FT], middle[0:NU].astype(BF16)).astype(BF16)
            ext_l[1][CC + c] = picked[0 : 2 * FT]
            ext_r[1][c] = picked[2 * FT : 4 * FT]
            w_v[c] = middle + x_v[c]
    for copy in halo(1):
        copy.start()
    sections(1)

    for copy in halo(1):
        copy.wait_recv()
    nothing = jnp.zeros((FT, LANES), BF16)
    for g in range(2):
        total = jnp.zeros((FT, LANES), F32)
        for b in range(4):
            c = 4 * g + b
            now = local_sweep(1, c, w_v[c], nothing)
            t_v[c] = now
            total = packed(1, b, now, total)
        a_s[1, :, LANES * g : LANES * g + LANES] = total.astype(BF16)
    send_ends(1)
    take_ends(1)
    same = (
        lax.broadcasted_iota(jnp.int32, (LANES, LANES), 0)
        == lax.broadcasted_iota(jnp.int32, (LANES, LANES), 1)
    ).astype(BF16)
    for g in range(2):
        entering = incoming(1, g)
        for b in range(4):
            c = 4 * g + b
            result = corrected(1, c, b, entering)[0:NU].astype(BF16)
            out_v[:, c] = nt(same, result).astype(BF16).reshape(NP, R, NU)

    for sweep in (0, 1):
        for copy in halo(sweep):
            copy.wait_send()
        for step in (1, 2, 3):

            @pl.when(a_sends(sweep, step))
            def _():
                a_copy(sweep, step).wait_send()

        for step in (1, 2):

            @pl.when(m_sends(sweep, step))
            def _():
                m_copy(sweep, step).wait_send()

    @pl.when(s > 0)
    def _():
        up_copy.wait_send()


def local(crosses, right_sides, initial, inverse_blocks, couplings, neighbours):
    hbm = pl.BlockSpec(memory_space=pltpu.HBM)
    vmem = pltpu.VMEM
    dma = pltpu.SemaphoreType.DMA
    return pl.pallas_call(
        functools.partial(kernel, crosses),
        out_shape=jax.ShapeDtypeStruct(right_sides.shape, BF16),
        in_specs=[
            pl.BlockSpec(memory_space=pltpu.SMEM),
            pl.BlockSpec(memory_space=pltpu.VMEM),
            hbm,
            hbm,
            hbm,
            hbm,
        ],
        out_specs=pl.BlockSpec(memory_space=pltpu.VMEM),
        scratch_shapes=[
            vmem((NP, CC, R, NU), BF16),
            vmem((NP, CC, R, NU), BF16),
            vmem((NP, NU, CC, NU), BF16),
            vmem((NP, 6, NT, CC, NU), BF16),
            vmem((2, 27, 16 * CC, 128), F32),
            vmem((CC, NP, NUP, NU), BF16),
            vmem((CC, NP, LOWER + FT, NU), BF16),
            vmem((CC, NP, NUP, LOWER + FT), BF16),
            vmem((2, CC, NUP, FT), F32),
            vmem((CC, NUP, LANES), F32),
            vmem((CC, NUP, LANES), F32),
            vmem((CC, NUP, LANES), F32),
            vmem((CC, FT, LANES), F32),
            vmem((CC, FT, LANES), F32),
            vmem((2, CC, NP, FT, FT), F32),
            vmem((2, CC, 3 * FT, FT), BF16),
            vmem((2, CC, 2 * FT, FT), BF16),
            vmem((2, CC, FT, FT), BF16),
            vmem((2, CC, 3 * FT, FT), BF16),
            vmem((2 * CC, 2 * FT, LANES), BF16),
            vmem((2 * CC, 2 * FT, LANES), BF16),
            vmem((2 * CC, 2 * FT, LANES), BF16),
            vmem((2 * CC, 2 * FT, LANES), BF16),
            vmem((FT, CC * R), BF16),
            vmem((FT, CC * R), BF16),
            vmem((2, FT, CC * R), BF16),
            vmem((2, 3, FT, CC * R), BF16),
            vmem((2, CC, FT, FT), BF16),
            vmem((2, 2, CC, FT, FT), BF16),
            dma((2,)),
            dma((2, NP)),
            dma((2, 2)),
            dma((2, 2)),
            dma((2,)),
            dma((2, 3)),
            dma((2, 3)),
            dma((2, 2)),
            dma((2, 2)),
        ],
        compiler_params=pltpu.CompilerParams(
            collective_id=0, has_side_effects=True, vmem_limit_bytes=56 * 1024 * 1024
        ),
        name="sweeps",
    )(
        neighbours.T,
        jnp.asarray(selector(), BF16),
        right_sides,
        initial,
        inverse_blocks.transpose(0, 2, 1, 3),
        couplings.transpose(0, 2, 3, 1, 4),
    )


def solution(mesh):
    return jax.shard_map(
        functools.partial(local, mesh.shape["cross"]),
        mesh=mesh,
        in_specs=(
            P("sweep", "cross", None, None),
            P("sweep", "cross", None, None),
            P("sweep", "cross", None, None),
            P("sweep", "cross", None, None, None),
            P("cross", None),
        ),
        out_specs=P("sweep", "cross", None, None),
        check_vma=False,
    )
```

```python
import functools

import jax
import jax.numpy as jnp
import numpy as np
from jax import lax
from jax.experimental import pallas as pl
from jax.experimental.pallas import tpu as pltpu
from jax.sharding import PartitionSpec as P

MESH = pl.DeviceIdType.MESH
NU, NT, R, CC, NP = 135, 45, 32, 8, 4
FT = 48
LANES = NP * R
NUP = 144
F32, BF16 = jnp.float32, jnp.bfloat16
WT = 80
STACK = (1, 2, 3, 4, 5)
NSTACK = len(STACK) * FT
LOWER = 256
CHUNK = 2


def selector():
    rows = np.zeros((2 * WT + 3 * FT, NU), np.float32)
    for half, which in enumerate((2, 0)):
        others = [node for node in range(3) if node != which]
        for v in range(5):
            for a in range(3):
                for b in range(3):
                    rows[half * WT + 9 * v + 3 * a + b, 27 * v + 9 * a + 3 * b + which] = 1.0
                for place, c in enumerate(others):
                    slot = NT + 6 * v + 2 * a + place
                    rows[half * WT + slot, 27 * v + 9 * a + 3 * which + c] = 1.0
                    rows[2 * WT + FT * (1 + half) + 9 * v + 3 * a + c, slot] = 1.0
                slot = 9 * v + 3 * a + which
                rows[2 * WT + FT * (1 + half) + slot, slot] = 1.0
    for v in range(5):
        rows[2 * WT + 9 * v : 2 * WT + 9 * v + 9, 27 * v : 27 * v + 9] = np.eye(9)
    return rows


def nn(a, b):
    return lax.dot_general(a, b, (((1,), (0,)), ((), ())), preferred_element_type=F32)


def nt(a, b):
    return lax.dot_general(a, b, (((1,), (1,)), ((), ())), preferred_element_type=F32)


def blocks(rows):
    return lax.broadcasted_iota(jnp.int32, (rows, LANES), 1) // R


def by_block(rows, parts):
    block = blocks(rows)
    total = parts[0][1]
    for b, part in parts[1:]:
        total = jnp.where(block == b, part, total)
    return total


def kernel(
    crosses,
    neigh_hbm,
    sel_hbm,
    rhs_hbm,
    init_hbm,
    inv_hbm,
    cpl_hbm,
    out_hbm,
    neigh,
    sel,
    init_v,
    rhs_v,
    out_v,
    inv_n,
    cpl_n,
    turn_v,
    inv_v,
    stack_v,
    d_v,
    rows_v,
    w_v,
    x_v,
    v_v,
    t_v,
    us_v,
    q_v,
    l1_v,
    l2_v,
    l3_v,
    e_v,
    mm_v,
    ext_l0,
    ext_l1,
    ext_r0,
    ext_r1,
    up_s,
    up_r,
    a_s,
    a_r,
    m_s,
    m_r,
    load_sem,
    plane_sem,
    out_sem,
    halo_s,
    halo_r,
    upsem,
    a_ss,
    a_rs,
    m_ss,
    m_rs,
):
    ext_l, ext_r = (ext_l0, ext_l1), (ext_r0, ext_r1)
    s = lax.axis_index("sweep")
    k = lax.axis_index("cross")
    right = lax.rem(k + 1, crosses)
    left = lax.rem(k + crosses - 1, crosses)

    load_init = pltpu.make_async_copy(init_hbm, init_v, load_sem.at[0])
    load_rhs = pltpu.make_async_copy(rhs_hbm, rhs_v, load_sem.at[1])

    def inv_load(p):
        return pltpu.make_async_copy(inv_hbm.at[p], inv_n.at[p], plane_sem.at[0, p])

    def cpl_load(p):
        return pltpu.make_async_copy(cpl_hbm.at[p], cpl_n.at[p], plane_sem.at[1, p])

    load_sel = pltpu.make_async_copy(sel_hbm, sel, load_sem.at[2])
    load_neigh = pltpu.make_async_copy(neigh_hbm, neigh, load_sem.at[3])
    load_sel.start()
    load_init.start()
    for p in range(NP):
        inv_load(p).start()
        cpl_load(p).start()
    load_rhs.start()
    load_neigh.start()

    barrier = pltpu.get_barrier_semaphore()
    for other in (left, right):
        pl.semaphore_signal(barrier, inc=1, device_id={"cross": other}, device_id_type=MESH)
    for step in (1, 2, 3):
        pl.semaphore_signal(
            barrier, inc=1, device_id={"sweep": lax.rem(s + step, 4)}, device_id_type=MESH
        )

    def halo(sweep, part):
        def copy(ext, direction, first, to, other):
            return pltpu.make_async_remote_copy(
                ext.at[pl.ds(first + CHUNK * part, CHUNK)],
                ext.at[pl.ds(to + CHUNK * part, CHUNK)],
                halo_s.at[sweep, direction, part],
                halo_r.at[sweep, direction, part],
                device_id={"cross": other},
                device_id_type=MESH,
            )

        return (
            copy(ext_l[sweep], 0, CC, 0, right),
            copy(ext_r[sweep], 1, 0, CC, left),
        )

    up_copy = pltpu.make_async_remote_copy(
        up_s,
        up_r,
        upsem.at[0],
        upsem.at[1],
        device_id={"sweep": lax.rem(s + 3, 4)},
        device_id_type=MESH,
    )

    load_sel.wait()
    load_init.wait()
    up_s[...] = nt(sel[2 * WT : 2 * WT + FT], init_v[0].reshape(CC * R, NU)).astype(BF16)
    for c in range(CC):
        picked = nt(sel[0 : 2 * WT + FT, 0:NU], init_v[:, c].reshape(LANES, NU))
        ext_l[0][CC + c] = picked[0:WT].astype(BF16)
        ext_r[0][c] = picked[WT : 2 * WT].astype(BF16)
        us_v[c] = pltpu.roll(picked[2 * WT : 2 * WT + FT], LANES - R, 1)
        if c == CHUNK - 1:
            pl.semaphore_wait(barrier, 5)
        if c % CHUNK == CHUNK - 1:
            for copy in halo(0, c // CHUNK):
                copy.start()

    @pl.when(s > 0)
    def _():
        up_copy.start()

    def a_copy(sweep, step):
        to = lax.rem(s + step, 4) if sweep == 0 else lax.rem(s + 4 - step, 4)
        return pltpu.make_async_remote_copy(
            a_s.at[sweep],
            a_r.at[sweep, step - 1],
            a_ss.at[sweep, step - 1],
            a_rs.at[sweep, step - 1],
            device_id={"sweep": to},
            device_id_type=MESH,
        )

    def m_copy(sweep, step):
        to = lax.rem(s + step, 4) if sweep == 0 else lax.rem(s + 4 - step, 4)
        return pltpu.make_async_remote_copy(
            m_s.at[sweep],
            m_r.at[sweep, step - 1],
            m_ss.at[sweep, step - 1],
            m_rs.at[sweep, step - 1],
            device_id={"sweep": to},
            device_id_type=MESH,
        )

    def a_sends(sweep, step):
        return s + step < 4 if sweep == 0 else s >= step

    def a_takes(sweep, step):
        return s >= step if sweep == 0 else s + step < 4

    def m_sends(sweep, step):
        if sweep == 0:
            return jnp.logical_and(s >= 1, s + step < 4)
        return jnp.logical_and(s <= 2, s >= step)

    def m_takes(sweep, step):
        return s >= step + 1 if sweep == 0 else s + step <= 2

    @pl.when(s == 3)
    def _():
        up_r[...] = jnp.zeros_like(up_r)

    for step in (1, 2, 3):

        @pl.when(s < step)
        def _():
            a_r[0, step - 1] = jnp.zeros((FT, CC * R), BF16)

        @pl.when(s + step > 3)
        def _():
            a_r[1, step - 1] = jnp.zeros((FT, CC * R), BF16)

    for step in (1, 2):

        @pl.when(s < step + 1)
        def _():
            m_r[0, step - 1] = jnp.zeros((CC, FT, FT), BF16)

        @pl.when(s + step > 2)
        def _():
            m_r[1, step - 1] = jnp.zeros((CC, FT, FT), BF16)

    inv_v[:, :, NU - 7 : NUP] = jnp.zeros((CC, NP, NUP - NU + 7, NU), BF16)
    for place in list(range(len(STACK))) + [LOWER // FT]:
        top = LOWER if place == LOWER // FT else FT * place
        stack_v[:, :, top + 32 : top + FT] = jnp.zeros((CC, NP, 16, NU), BF16)
    stack_v[:, :, NSTACK:LOWER] = jnp.zeros((CC, NP, LOWER - NSTACK, NU), BF16)
    q_v[...] = jnp.zeros_like(q_v)

    def turn(slot, block, count, to, p, first):
        flat = block.astype(F32).reshape(CC * count, NU)
        turn_v[0, slot, 0 : CC * count] = flat[:, 0:128]
        turn_v[1, slot, 0 : CC * count, 0 : NU - 128] = flat[:, 128:NU]
        for c in range(CC):
            rows = pl.ds(c, count, stride=CC)
            to[c, p, first : first + count, 0:128] = turn_v[0, slot, rows].astype(BF16)
            to[c, p, first : first + count, 128:NU] = turn_v[1, slot, rows][
                :, 0 : NU - 128
            ].astype(BF16)

    def products(p, carry):
        inv_load(p).wait()
        cpl_load(p).wait()
        slot = 0
        for first in range(0, NU, 16):
            count = min(16, NU - first)
            turn(slot, inv_n[p, first : first + count], count, inv_v, p, first)
            slot += 1
        for top, face in [(FT * place, face) for place, face in enumerate(STACK)] + [(LOWER, 0)]:
            for first in range(0, NT, 16):
                count = min(16, NT - first)
                block = cpl_n[p, face, first : first + count]
                turn(slot, block, count, stack_v, p, top + first)
                slot += 1
        for c in range(CC):
            d = nt(inv_v[c, p], stack_v[c, p])
            d_v[c, p] = d.astype(BF16)
            rows_v[0, c] = d[:, LOWER : LOWER + FT]
            rows_v[1, c] = d[:, 0:FT]
            for var in range(5):
                to = slice(9 * var, 9 * var + 9)
                q_v[0, c, p, to] = rows_v[0, c, 27 * var + 18 : 27 * var + 27]
                q_v[1, c, p, to] = rows_v[1, c, 27 * var : 27 * var + 9]
        return carry

    lax.fori_loop(0, NP, products, 0)
    load_rhs.wait()

    def by_plane(rows, stacked):
        return by_block(rows, [(p, stacked[rows * p : rows * p + rows]) for p in range(NP)])

    for c in range(CC):
        rhs = rhs_v[:, c].reshape(LANES, NU)
        w_v[c] = by_plane(NUP, nt(inv_v[c].reshape(NP * NUP, NU), rhs))

    def order_of(sweep):
        return list(range(NP)) if sweep == 0 else list(range(NP - 1, -1, -1))

    def d_in(sweep, c):
        low = LOWER if sweep == 0 else 0
        return d_v[c, :, :, low : low + FT]

    def sections(sweep):
        order = order_of(sweep)
        n = [[(-q_v[sweep, c, p]).astype(BF16) for p in order] for c in range(CC)]
        two = [
            [nn(n[c][o], n[c][o - 1]).astype(BF16) for o in (1, 2, 3)] for c in range(CC)
        ]
        for c in range(CC):
            for o in (1, 2, 3):
                l1_v[sweep, c, FT * (o - 1) : FT * o] = n[c][o]
            for o in (2, 3):
                l2_v[sweep, c, FT * (o - 2) : FT * (o - 1)] = two[c][o - 1]
            e_v[sweep, c, order[0]] = d_in(sweep, c)[order[0]]
            fronts = (n[c][0], two[c][0], nn(two[c][1], n[c][0]).astype(BF16))
            for o in (1, 2, 3):
                e_v[sweep, c, order[o]] = nn(d_in(sweep, c)[order[o]], fronts[o - 1]).astype(BF16)
            l3_v[sweep, c] = nn(two[c][2], n[c][1]).astype(BF16)
            m_s[sweep, c] = nn(two[c][2], two[c][0]).astype(BF16)
        for step in (1, 2):

            @pl.when(m_sends(sweep, step))
            def _():
                m_copy(sweep, step).start()

    sections(0)

    def gathered(sweep, c, upper):
        low = lax.rem(neigh[2, c] - (k - 1) * CC + 2 * crosses * CC, crosses * CC)
        high = lax.rem(neigh[3, c] - k * CC + crosses * CC, crosses * CC)
        low = jnp.clip(low, 0, 2 * CC - 1)
        high = jnp.clip(high, 0, 2 * CC - 1)
        apart = [sel[2 * WT + FT * half : 2 * WT + FT * half + FT, 0:WT] for half in (1, 2)]
        return jnp.concatenate(
            [
                upper,
                nn(apart[0], ext_l[sweep][c]).astype(BF16),
                nn(apart[1], ext_r[sweep][CC + c]).astype(BF16),
                ext_l[sweep][low, 0:FT],
                ext_r[sweep][high, 0:FT],
            ],
            axis=0,
        )

    def shift_of(sweep, steps):
        return R * steps if sweep == 0 else LANES - R * steps

    def local_sweep(sweep, c, base, upper):
        order = order_of(sweep)
        stack = gathered(sweep, c, upper)
        x = by_plane(NUP, nn(d_v[c].reshape(NP * NUP, LOWER + FT)[:, 0:NSTACK], stack))
        v = base - x
        v_v[c] = v
        if sweep == 0:
            x_v[c] = x
        start = 18 if sweep == 0 else 0
        pieces = [v_v[c, 27 * var + start : 27 * var + start + 9] for var in range(5)]
        for var in range(5):
            t_v[c, 9 * var : 9 * var + 9] = pieces[var]
        u = t_v[c]
        block = blocks(FT)
        total = u
        for steps, left_v in ((1, l1_v), (2, l2_v), (3, l3_v)):
            moved = pltpu.roll(u, shift_of(sweep, steps), 1).astype(BF16)
            z = nn(left_v[sweep, c], moved)
            for o in range(steps, NP):
                part = z[FT * (o - steps) : FT * (o - steps + 1)]
                total = total + jnp.where(block == order[o], part, 0.0)
        return total

    def packed(sweep, b, now, total):
        last = 3 if sweep == 0 else 0
        turned_in = now if b == last else pltpu.roll(now, (R * (b - last)) % LANES, 1)
        return jnp.where(blocks(FT) == b, turned_in, total)

    def spread(b, group):
        one = jnp.where(blocks(FT) == b, group, 0.0)
        one = one + pltpu.roll(one, R, 1)
        return one + pltpu.roll(one, 2 * R, 1)

    def send_ends(sweep):
        for step in (1, 2, 3):

            @pl.when(a_sends(sweep, step))
            def _():
                a_copy(sweep, step).start()

    def rest_of_sweep(sweep):
        order = order_of(sweep)
        for c in range(CC):
            moved = pltpu.roll(t_v[c], shift_of(sweep, 1), 1)
            before = jnp.where(blocks(FT) == order[0], 0.0, moved).astype(BF16)
            y = nn(d_in(sweep, c).reshape(NP * NUP, FT), before)
            v_v[c] = v_v[c] - by_plane(NUP, y)
        for step in (1, 2):

            @pl.when(m_takes(sweep, step))
            def _():
                m_copy(sweep, step).wait_recv()

        for c in range(CC):
            mm_v[c] = nn(m_r[sweep, 0, c], m_r[sweep, 1, c]).astype(BF16)

    def take_ends(sweep):
        for step in (1, 2, 3):

            @pl.when(a_takes(sweep, step))
            def _():
                a_copy(sweep, step).wait_recv()

    def incoming(sweep, g):
        lanes = slice(LANES * g, LANES * g + LANES)
        parts = []
        for b in range(4):
            c = 4 * g + b
            one = nn(m_r[sweep, 0, c], a_r[sweep, 1, :, lanes])
            parts.append((b, one + nn(mm_v[c], a_r[sweep, 2, :, lanes])))
        return a_r[sweep, 0, :, lanes].astype(F32) + by_block(FT, parts)

    def corrected(sweep, c, b, entering):
        t = spread(b, entering).astype(BF16)
        return v_v[c] - by_plane(NUP, nn(e_v[sweep, c].reshape(NP * NUP, FT), t))

    load_neigh.wait()
    for part in range(CC // CHUNK):
        for copy in halo(0, part):
            copy.wait_recv()

    @pl.when(s < 3)
    def _():
        up_copy.wait_recv()

    t_v[...] = jnp.zeros_like(t_v)
    for g in range(2):
        total = jnp.zeros((FT, LANES), F32)
        for b in range(4):
            c = 4 * g + b
            edge = up_r[:, LANES * g : LANES * g + LANES].astype(F32)
            edge = pltpu.roll(edge, (R * (3 - b)) % LANES, 1) if b != 3 else edge
            upper = jnp.where(blocks(FT) == 3, edge, us_v[c]).astype(BF16)
            now = local_sweep(0, c, w_v[c], upper)
            t_v[c] = now
            total = packed(0, b, now, total)
        a_s[0, :, LANES * g : LANES * g + LANES] = total.astype(BF16)
    send_ends(0)
    rest_of_sweep(0)
    take_ends(0)
    for g in range(2):
        entering = incoming(0, g)
        for b in range(4):
            c = 4 * g + b
            middle = corrected(0, c, b, entering)
            picked = nn(sel[0 : 2 * WT, 0:NU], middle[0:NU].astype(BF16)).astype(BF16)
            ext_l[1][CC + c] = picked[0:WT]
            ext_r[1][c] = picked[WT : 2 * WT]
            if c % CHUNK == CHUNK - 1:
                for copy in halo(1, c // CHUNK):
                    copy.start()
            w_v[c] = middle + x_v[c]
    sections(1)

    for part in range(CC // CHUNK):
        for copy in halo(1, part):
            copy.wait_recv()
    nothing = jnp.zeros((FT, LANES), BF16)
    for g in range(2):
        total = jnp.zeros((FT, LANES), F32)
        for b in range(4):
            c = 4 * g + b
            now = local_sweep(1, c, w_v[c], nothing)
            t_v[c] = now
            total = packed(1, b, now, total)
        a_s[1, :, LANES * g : LANES * g + LANES] = total.astype(BF16)
    send_ends(1)
    rest_of_sweep(1)
    take_ends(1)

    def out_store(c):
        return pltpu.make_async_copy(out_v.at[:, c], out_hbm.at[:, c], out_sem.at[c])

    same = (
        lax.broadcasted_iota(jnp.int32, (LANES, LANES), 0)
        == lax.broadcasted_iota(jnp.int32, (LANES, LANES), 1)
    ).astype(BF16)
    for g in range(2):
        entering = incoming(1, g)
        for b in range(4):
            c = 4 * g + b
            result = corrected(1, c, b, entering)[0:NU].astype(BF16)
            out_v[:, c] = nt(same, result).astype(BF16).reshape(NP, R, NU)
            out_store(c).start()
    for c in range(CC):
        out_store(c).wait()

    for sweep in (0, 1):
        for part in range(CC // CHUNK):
            for copy in halo(sweep, part):
                copy.wait_send()
        for step in (1, 2, 3):

            @pl.when(a_sends(sweep, step))
            def _():
                a_copy(sweep, step).wait_send()

        for step in (1, 2):

            @pl.when(m_sends(sweep, step))
            def _():
                m_copy(sweep, step).wait_send()

    @pl.when(s > 0)
    def _():
        up_copy.wait_send()


def local(crosses, right_sides, initial, inverse_blocks, couplings, neighbours):
    hbm = pl.BlockSpec(memory_space=pltpu.HBM)
    vmem = pltpu.VMEM
    dma = pltpu.SemaphoreType.DMA
    return pl.pallas_call(
        functools.partial(kernel, crosses),
        out_shape=jax.ShapeDtypeStruct(right_sides.shape, BF16),
        in_specs=[
            hbm,
            hbm,
            hbm,
            hbm,
            hbm,
            hbm,
        ],
        out_specs=pl.BlockSpec(memory_space=pl.ANY),
        scratch_shapes=[
            pltpu.SMEM((4, CC), jnp.int32),
            vmem((2 * WT + 3 * FT, NU), BF16),
            vmem((NP, CC, R, NU), BF16),
            vmem((NP, CC, R, NU), BF16),
            vmem((NP, CC, R, NU), BF16),
            vmem((NP, NU, CC, NU), BF16),
            vmem((NP, 6, NT, CC, NU), BF16),
            vmem((2, 27, 16 * CC, 128), F32),
            vmem((CC, NP, NUP, NU), BF16),
            vmem((CC, NP, LOWER + FT, NU), BF16),
            vmem((CC, NP, NUP, LOWER + FT), BF16),
            vmem((2, CC, NUP, FT), F32),
            vmem((CC, NUP, LANES), F32),
            vmem((CC, NUP, LANES), F32),
            vmem((CC, NUP, LANES), F32),
            vmem((CC, FT, LANES), F32),
            vmem((CC, FT, LANES), F32),
            vmem((2, CC, NP, FT, FT), F32),
            vmem((2, CC, 3 * FT, FT), BF16),
            vmem((2, CC, 2 * FT, FT), BF16),
            vmem((2, CC, FT, FT), BF16),
            vmem((2, CC, NP, NUP, FT), BF16),
            vmem((CC, FT, FT), BF16),
            vmem((2 * CC, WT, LANES), BF16),
            vmem((2 * CC, WT, LANES), BF16),
            vmem((2 * CC, WT, LANES), BF16),
            vmem((2 * CC, WT, LANES), BF16),
            vmem((FT, CC * R), BF16),
            vmem((FT, CC * R), BF16),
            vmem((2, FT, CC * R), BF16),
            vmem((2, 3, FT, CC * R), BF16),
            vmem((2, CC, FT, FT), BF16),
            vmem((2, 2, CC, FT, FT), BF16),
            dma((4,)),
            dma((2, NP)),
            dma((CC,)),
            dma((2, 2, CC // CHUNK)),
            dma((2, 2, CC // CHUNK)),
            dma((2,)),
            dma((2, 3)),
            dma((2, 3)),
            dma((2, 2)),
            dma((2, 2)),
        ],
        compiler_params=pltpu.CompilerParams(
            collective_id=0, has_side_effects=True, vmem_limit_bytes=56 * 1024 * 1024
        ),
        name="sweeps",
    )(
        neighbours.T,
        jnp.asarray(selector(), BF16),
        right_sides,
        initial,
        inverse_blocks.transpose(0, 2, 1, 3),
        couplings.transpose(0, 2, 3, 1, 4),
    )


def solution(mesh):
    return jax.shard_map(
        functools.partial(local, mesh.shape["cross"]),
        mesh=mesh,
        in_specs=(
            P("sweep", "cross", None, None),
            P("sweep", "cross", None, None),
            P("sweep", "cross", None, None),
            P("sweep", "cross", None, None, None),
            P("cross", None),
        ),
        out_specs=P("sweep", "cross", None, None),
        check_vma=False,
    )
```

```python
import functools

import jax
import jax.numpy as jnp
import numpy as np
from jax import lax
from jax.experimental import pallas as pl
from jax.experimental.pallas import tpu as pltpu
from jax.sharding import PartitionSpec as P

MESH = pl.DeviceIdType.MESH
NU, NT, R, CC, NP = 135, 45, 32, 8, 4
FT = 48
LANES = NP * R
NUP = 144
F32, BF16 = jnp.float32, jnp.bfloat16
WT = 80
STACK = (1, 2, 3, 4, 5)
NSTACK = len(STACK) * FT
LOWER = 256
CHUNK = 2


def selector():
    rows = np.zeros((2 * WT + 3 * FT, NU), np.float32)
    for half, which in enumerate((2, 0)):
        others = [node for node in range(3) if node != which]
        for v in range(5):
            for a in range(3):
                for b in range(3):
                    rows[half * WT + 9 * v + 3 * a + b, 27 * v + 9 * a + 3 * b + which] = 1.0
                for place, c in enumerate(others):
                    slot = NT + 6 * v + 2 * a + place
                    rows[half * WT + slot, 27 * v + 9 * a + 3 * which + c] = 1.0
                    rows[2 * WT + FT * (1 + half) + 9 * v + 3 * a + c, slot] = 1.0
                slot = 9 * v + 3 * a + which
                rows[2 * WT + FT * (1 + half) + slot, slot] = 1.0
    for v in range(5):
        rows[2 * WT + 9 * v : 2 * WT + 9 * v + 9, 27 * v : 27 * v + 9] = np.eye(9)
    return rows


def nn(a, b):
    return lax.dot_general(a, b, (((1,), (0,)), ((), ())), preferred_element_type=F32)


def nt(a, b):
    return lax.dot_general(a, b, (((1,), (1,)), ((), ())), preferred_element_type=F32)


def blocks(rows):
    return lax.broadcasted_iota(jnp.int32, (rows, LANES), 1) // R


def by_block(rows, parts):
    block = blocks(rows)
    total = parts[0][1]
    for b, part in parts[1:]:
        total = jnp.where(block == b, part, total)
    return total


def kernel(
    crosses,
    neigh_hbm,
    sel_hbm,
    rhs_hbm,
    init_hbm,
    inv_hbm,
    cpl_hbm,
    out_hbm,
    neigh,
    sel,
    init_v,
    rhs_v,
    out_v,
    inv_n,
    cpl_n,
    turn_v,
    inv_v,
    stack_v,
    d_v,
    rows_v,
    w_v,
    x_v,
    v_v,
    t_v,
    us_v,
    q_v,
    face_v,
    col_v,
    u_v,
    w_face_v,
    l1_v,
    l2_v,
    l3_v,
    e_v,
    mm_v,
    ext_l0,
    ext_l1,
    ext_r0,
    ext_r1,
    up_s,
    up_r,
    a_s,
    a_r,
    m_s,
    m_r,
    load_sem,
    plane_sem,
    out_sem,
    halo_s,
    halo_r,
    upsem,
    a_ss,
    a_rs,
    m_ss,
    m_rs,
):
    ext_l, ext_r = (ext_l0, ext_l1), (ext_r0, ext_r1)
    s = lax.axis_index("sweep")
    k = lax.axis_index("cross")
    right = lax.rem(k + 1, crosses)
    left = lax.rem(k + crosses - 1, crosses)

    load_init = pltpu.make_async_copy(init_hbm, init_v, load_sem.at[0])
    load_rhs = pltpu.make_async_copy(rhs_hbm, rhs_v, load_sem.at[1])

    def inv_load(p):
        return pltpu.make_async_copy(inv_hbm.at[p], inv_n.at[p], plane_sem.at[0, p])

    def cpl_load(p):
        return pltpu.make_async_copy(cpl_hbm.at[p], cpl_n.at[p], plane_sem.at[1, p])

    load_sel = pltpu.make_async_copy(sel_hbm, sel, load_sem.at[2])
    load_neigh = pltpu.make_async_copy(neigh_hbm, neigh, load_sem.at[3])
    load_sel.start()
    load_init.start()
    for p in range(NP):
        inv_load(p).start()
        cpl_load(p).start()
    load_rhs.start()
    load_neigh.start()

    barrier = pltpu.get_barrier_semaphore()
    for other in (left, right):
        pl.semaphore_signal(barrier, inc=1, device_id={"cross": other}, device_id_type=MESH)
    for step in (1, 2, 3):
        pl.semaphore_signal(
            barrier, inc=1, device_id={"sweep": lax.rem(s + step, 4)}, device_id_type=MESH
        )

    def halo(sweep, part):
        def copy(ext, direction, first, to, other):
            return pltpu.make_async_remote_copy(
                ext.at[pl.ds(first + CHUNK * part, CHUNK)],
                ext.at[pl.ds(to + CHUNK * part, CHUNK)],
                halo_s.at[sweep, direction, part],
                halo_r.at[sweep, direction, part],
                device_id={"cross": other},
                device_id_type=MESH,
            )

        return (
            copy(ext_l[sweep], 0, CC, 0, right),
            copy(ext_r[sweep], 1, 0, CC, left),
        )

    up_copy = pltpu.make_async_remote_copy(
        up_s,
        up_r,
        upsem.at[0],
        upsem.at[1],
        device_id={"sweep": lax.rem(s + 3, 4)},
        device_id_type=MESH,
    )

    load_sel.wait()
    load_init.wait()
    up_s[...] = nt(sel[2 * WT : 2 * WT + FT], init_v[0].reshape(CC * R, NU)).astype(BF16)
    for c in range(CC):
        picked = nt(sel[0 : 2 * WT + FT, 0:NU], init_v[:, c].reshape(LANES, NU))
        ext_l[0][CC + c] = picked[0:WT].astype(BF16)
        ext_r[0][c] = picked[WT : 2 * WT].astype(BF16)
        us_v[c] = pltpu.roll(picked[2 * WT : 2 * WT + FT], LANES - R, 1)
        if c == CHUNK - 1:
            pl.semaphore_wait(barrier, 5)
        if c % CHUNK == CHUNK - 1:
            for copy in halo(0, c // CHUNK):
                copy.start()

    @pl.when(s > 0)
    def _():
        up_copy.start()

    def a_copy(sweep, step):
        to = lax.rem(s + step, 4) if sweep == 0 else lax.rem(s + 4 - step, 4)
        return pltpu.make_async_remote_copy(
            a_s.at[sweep],
            a_r.at[sweep, step - 1],
            a_ss.at[sweep, step - 1],
            a_rs.at[sweep, step - 1],
            device_id={"sweep": to},
            device_id_type=MESH,
        )

    def m_copy(sweep, step):
        to = lax.rem(s + step, 4) if sweep == 0 else lax.rem(s + 4 - step, 4)
        return pltpu.make_async_remote_copy(
            m_s.at[sweep],
            m_r.at[sweep, step - 1],
            m_ss.at[sweep, step - 1],
            m_rs.at[sweep, step - 1],
            device_id={"sweep": to},
            device_id_type=MESH,
        )

    def a_sends(sweep, step):
        return s + step < 4 if sweep == 0 else s >= step

    def a_takes(sweep, step):
        return s >= step if sweep == 0 else s + step < 4

    def m_sends(sweep, step):
        if sweep == 0:
            return jnp.logical_and(s >= 1, s + step < 4)
        return jnp.logical_and(s <= 2, s >= step)

    def m_takes(sweep, step):
        return s >= step + 1 if sweep == 0 else s + step <= 2

    @pl.when(s == 3)
    def _():
        up_r[...] = jnp.zeros_like(up_r)

    for step in (1, 2, 3):

        @pl.when(s < step)
        def _():
            a_r[0, step - 1] = jnp.zeros((FT, CC * R), BF16)

        @pl.when(s + step > 3)
        def _():
            a_r[1, step - 1] = jnp.zeros((FT, CC * R), BF16)

    for step in (1, 2):

        @pl.when(s < step + 1)
        def _():
            m_r[0, step - 1] = jnp.zeros((CC, FT, FT), BF16)

        @pl.when(s + step > 2)
        def _():
            m_r[1, step - 1] = jnp.zeros((CC, FT, FT), BF16)

    inv_v[:, :, NU - 7 : NUP] = jnp.zeros((CC, NP, NUP - NU + 7, NU), BF16)
    for place in list(range(len(STACK))) + [LOWER // FT]:
        top = LOWER if place == LOWER // FT else FT * place
        stack_v[:, :, top + 32 : top + FT] = jnp.zeros((CC, NP, 16, NU), BF16)
    stack_v[:, :, NSTACK:LOWER] = jnp.zeros((CC, NP, LOWER - NSTACK, NU), BF16)
    q_v[...] = jnp.zeros_like(q_v)
    for rows in (u_v, w_face_v):
        rows[:, 40:FT] = jnp.zeros((CC, FT - 40, LANES), F32)

    def turn(slot, block, count, to, p, first):
        flat = block.astype(F32).reshape(CC * count, NU)
        turn_v[0, slot, 0 : CC * count] = flat[:, 0:128]
        turn_v[1, slot, 0 : CC * count, 0 : NU - 128] = flat[:, 128:NU]
        for c in range(CC):
            rows = pl.ds(c, count, stride=CC)
            to[c, p, first : first + count, 0:128] = turn_v[0, slot, rows].astype(BF16)
            to[c, p, first : first + count, 128:NU] = turn_v[1, slot, rows][
                :, 0 : NU - 128
            ].astype(BF16)

    def products(p, carry):
        inv_load(p).wait()
        cpl_load(p).wait()
        slot = 0
        for first in range(0, NU, 16):
            count = min(16, NU - first)
            turn(slot, inv_n[p, first : first + count], count, inv_v, p, first)
            slot += 1
        for top, face in [(FT * place, face) for place, face in enumerate(STACK)] + [(LOWER, 0)]:
            for first in range(0, NT, 16):
                count = min(16, NT - first)
                block = cpl_n[p, face, first : first + count]
                turn(slot, block, count, stack_v, p, top + first)
                slot += 1
        for c in range(CC):
            d = nt(inv_v[c, p], stack_v[c, p])
            d_v[c, p] = d.astype(BF16)
            rows_v[c] = d[:, LOWER : LOWER + FT]
            for var in range(5):
                to = slice(9 * var, 9 * var + 9)
                q_v[c, p, to] = rows_v[c, 27 * var + 18 : 27 * var + 27]
        return carry

    lax.fori_loop(0, NP, products, 0)
    load_rhs.wait()

    def by_plane(rows, stacked):
        return by_block(rows, [(p, stacked[rows * p : rows * p + rows]) for p in range(NP)])

    for c in range(CC):
        rhs = rhs_v[:, c].reshape(LANES, NU)
        w_v[c] = by_plane(NUP, nt(inv_v[c].reshape(NP * NUP, NU), rhs))

    def order_of(sweep):
        return list(range(NP)) if sweep == 0 else list(range(NP - 1, -1, -1))

    def d_in(sweep, c):
        low = LOWER if sweep == 0 else 0
        return d_v[c, :, :, low : low + FT]

    def sections(sweep):
        order = order_of(sweep)
        if sweep == 0:
            n = [[(-q_v[c, p]).astype(BF16) for p in order] for c in range(CC)]
        else:
            n = [[-face_v[c, p, :, 0:FT] for p in order] for c in range(CC)]
        two = [
            [nn(n[c][o], n[c][o - 1]).astype(BF16) for o in (1, 2, 3)] for c in range(CC)
        ]
        for c in range(CC):
            for o in (1, 2, 3):
                l1_v[sweep, c, FT * (o - 1) : FT * o] = n[c][o]
            for o in (2, 3):
                l2_v[sweep, c, FT * (o - 2) : FT * (o - 1)] = two[c][o - 1]
            e_v[sweep, c, order[0]] = d_in(sweep, c)[order[0]]
            fronts = (n[c][0], two[c][0], nn(two[c][1], n[c][0]).astype(BF16))
            for o in (1, 2, 3):
                e_v[sweep, c, order[o]] = nn(d_in(sweep, c)[order[o]], fronts[o - 1]).astype(BF16)
            l3_v[sweep, c] = nn(two[c][2], n[c][1]).astype(BF16)
            m_s[sweep, c] = nn(two[c][2], two[c][0]).astype(BF16)
        for step in (1, 2):

            @pl.when(m_sends(sweep, step))
            def _():
                m_copy(sweep, step).start()

    sections(0)

    def gathered(sweep, c, upper):
        low = lax.rem(neigh[2, c] - (k - 1) * CC + 2 * crosses * CC, crosses * CC)
        high = lax.rem(neigh[3, c] - k * CC + crosses * CC, crosses * CC)
        low = jnp.clip(low, 0, 2 * CC - 1)
        high = jnp.clip(high, 0, 2 * CC - 1)
        apart = [sel[2 * WT + FT * half : 2 * WT + FT * half + FT, 0:WT] for half in (1, 2)]
        col_v[c, 0:FT] = upper
        col_v[c, FT : 2 * FT] = nn(apart[0], ext_l[sweep][c]).astype(BF16)
        col_v[c, 2 * FT : 3 * FT] = nn(apart[1], ext_r[sweep][CC + c]).astype(BF16)
        col_v[c, 3 * FT : 4 * FT] = ext_l[sweep][low, 0:FT]
        col_v[c, 4 * FT : 5 * FT] = ext_r[sweep][high, 0:FT]

    def shift_of(sweep, steps):
        return R * steps if sweep == 0 else LANES - R * steps

    def applied_to_column(c):
        d = d_v[c].reshape(NP * NUP, LOWER + FT)[:, 0:NSTACK]
        return by_plane(NUP, nn(d, col_v[c]))

    def local_faces(sweep):
        order = order_of(sweep)
        block = blocks(FT)
        for c in range(CC):
            total = u_v[c]
            for steps, left_v in ((1, l1_v), (2, l2_v), (3, l3_v)):
                moved = pltpu.roll(u_v[c], shift_of(sweep, steps), 1).astype(BF16)
                z = nn(left_v[sweep, c], moved)
                for o in range(steps, NP):
                    part = z[FT * (o - steps) : FT * (o - steps + 1)]
                    total = total + jnp.where(block == order[o], part, 0.0)
            t_v[c] = total
        for g in range(2):
            total = jnp.zeros((FT, LANES), F32)
            for b in range(4):
                total = packed(sweep, b, t_v[4 * g + b], total)
            a_s[sweep, :, LANES * g : LANES * g + LANES] = total.astype(BF16)

    def before_of(sweep, c):
        moved = pltpu.roll(t_v[c], shift_of(sweep, 1), 1)
        return jnp.where(blocks(FT) == order_of(sweep)[0], 0.0, moved).astype(BF16)

    def packed(sweep, b, now, total):
        last = 3 if sweep == 0 else 0
        turned_in = now if b == last else pltpu.roll(now, (R * (b - last)) % LANES, 1)
        return jnp.where(blocks(FT) == b, turned_in, total)

    def spread(b, group):
        one = jnp.where(blocks(FT) == b, group, 0.0)
        one = one + pltpu.roll(one, R, 1)
        return one + pltpu.roll(one, 2 * R, 1)

    def send_ends(sweep):
        for step in (1, 2, 3):

            @pl.when(a_sends(sweep, step))
            def _():
                a_copy(sweep, step).start()

    def take_operators(sweep):
        for step in (1, 2):

            @pl.when(m_takes(sweep, step))
            def _():
                m_copy(sweep, step).wait_recv()

        for c in range(CC):
            mm_v[c] = nn(m_r[sweep, 0, c], m_r[sweep, 1, c]).astype(BF16)

    def take_ends(sweep):
        for step in (1, 2, 3):

            @pl.when(a_takes(sweep, step))
            def _():
                a_copy(sweep, step).wait_recv()

    def incoming(sweep, g):
        lanes = slice(LANES * g, LANES * g + LANES)
        parts = []
        for b in range(4):
            c = 4 * g + b
            one = nn(m_r[sweep, 0, c], a_r[sweep, 1, :, lanes])
            parts.append((b, one + nn(mm_v[c], a_r[sweep, 2, :, lanes])))
        return a_r[sweep, 0, :, lanes].astype(F32) + by_block(FT, parts)

    def corrected(sweep, c, b, entering):
        t = spread(b, entering).astype(BF16)
        return v_v[c] - by_plane(NUP, nn(e_v[sweep, c].reshape(NP * NUP, FT), t))

    load_neigh.wait()
    for part in range(CC // CHUNK):
        for copy in halo(0, part):
            copy.wait_recv()

    @pl.when(s < 3)
    def _():
        up_copy.wait_recv()

    for c in range(CC):
        g, b = c // 4, c % 4
        edge = up_r[:, LANES * g : LANES * g + LANES].astype(F32)
        edge = pltpu.roll(edge, (R * (3 - b)) % LANES, 1) if b != 3 else edge
        gathered(0, c, jnp.where(blocks(FT) == 3, edge, us_v[c]).astype(BF16))
    for c in range(CC):
        x = applied_to_column(c)
        x_v[c] = x
        v_v[c] = w_v[c] - x
        for var in range(5):
            u_v[c, 9 * var : 9 * var + 9] = v_v[c, 27 * var + 18 : 27 * var + 27]
    local_faces(0)
    send_ends(0)
    for c in range(CC):
        y = nn(d_in(0, c).reshape(NP * NUP, FT), before_of(0, c))
        v_v[c] = v_v[c] - by_plane(NUP, y)
    take_operators(0)
    take_ends(0)
    for g in range(2):
        entering = incoming(0, g)
        for b in range(4):
            c = 4 * g + b
            middle = corrected(0, c, b, entering)
            picked = nn(sel[0 : 2 * WT, 0:NU], middle[0:NU].astype(BF16)).astype(BF16)
            ext_l[1][CC + c] = picked[0:WT]
            ext_r[1][c] = picked[WT : 2 * WT]
            if c % CHUNK == CHUNK - 1:
                for copy in halo(1, c // CHUNK):
                    copy.start()
            w_v[c] = middle + x_v[c]
    for c in range(CC):
        for p in range(NP):
            face_v[c, p] = nn(sel[2 * WT : 2 * WT + FT], d_v[c, p, 0:NU, 0:NSTACK]).astype(BF16)
        for var in range(5):
            w_face_v[c, 9 * var : 9 * var + 9] = w_v[c, 27 * var : 27 * var + 9]
    sections(1)

    for part in range(CC // CHUNK):
        for copy in halo(1, part):
            copy.wait_recv()
    for c in range(CC):
        gathered(1, c, jnp.zeros((FT, LANES), BF16))
    for c in range(CC):
        faces = face_v[c].reshape(NP * FT, NSTACK)
        u_v[c] = w_face_v[c] - by_plane(FT, nn(faces, col_v[c]))
    local_faces(1)
    send_ends(1)
    for c in range(CC):
        col_v[c, 0:FT] = before_of(1, c)
    for c in range(CC):
        v_v[c] = w_v[c] - applied_to_column(c)
    take_operators(1)
    take_ends(1)

    def out_store(c):
        return pltpu.make_async_copy(out_v.at[:, c], out_hbm.at[:, c], out_sem.at[c])

    same = (
        lax.broadcasted_iota(jnp.int32, (LANES, LANES), 0)
        == lax.broadcasted_iota(jnp.int32, (LANES, LANES), 1)
    ).astype(BF16)
    for g in range(2):
        entering = incoming(1, g)
        for b in range(4):
            c = 4 * g + b
            result = corrected(1, c, b, entering)[0:NU].astype(BF16)
            out_v[:, c] = nt(same, result).astype(BF16).reshape(NP, R, NU)
            out_store(c).start()
    for c in range(CC):
        out_store(c).wait()

    for sweep in (0, 1):
        for part in range(CC // CHUNK):
            for copy in halo(sweep, part):
                copy.wait_send()
        for step in (1, 2, 3):

            @pl.when(a_sends(sweep, step))
            def _():
                a_copy(sweep, step).wait_send()

        for step in (1, 2):

            @pl.when(m_sends(sweep, step))
            def _():
                m_copy(sweep, step).wait_send()

    @pl.when(s > 0)
    def _():
        up_copy.wait_send()


def local(crosses, right_sides, initial, inverse_blocks, couplings, neighbours):
    hbm = pl.BlockSpec(memory_space=pltpu.HBM)
    vmem = pltpu.VMEM
    dma = pltpu.SemaphoreType.DMA
    return pl.pallas_call(
        functools.partial(kernel, crosses),
        out_shape=jax.ShapeDtypeStruct(right_sides.shape, BF16),
        in_specs=[
            hbm,
            hbm,
            hbm,
            hbm,
            hbm,
            hbm,
        ],
        out_specs=pl.BlockSpec(memory_space=pl.ANY),
        scratch_shapes=[
            pltpu.SMEM((4, CC), jnp.int32),
            vmem((2 * WT + 3 * FT, NU), BF16),
            vmem((NP, CC, R, NU), BF16),
            vmem((NP, CC, R, NU), BF16),
            vmem((NP, CC, R, NU), BF16),
            vmem((NP, NU, CC, NU), BF16),
            vmem((NP, 6, NT, CC, NU), BF16),
            vmem((2, 27, 16 * CC, 128), F32),
            vmem((CC, NP, NUP, NU), BF16),
            vmem((CC, NP, LOWER + FT, NU), BF16),
            vmem((CC, NP, NUP, LOWER + FT), BF16),
            vmem((CC, NUP, FT), F32),
            vmem((CC, NUP, LANES), F32),
            vmem((CC, NUP, LANES), F32),
            vmem((CC, NUP, LANES), F32),
            vmem((CC, FT, LANES), F32),
            vmem((CC, FT, LANES), F32),
            vmem((CC, NP, FT, FT), F32),
            vmem((CC, NP, FT, NSTACK), BF16),
            vmem((CC, NSTACK, LANES), BF16),
            vmem((CC, FT, LANES), F32),
            vmem((CC, FT, LANES), F32),
            vmem((2, CC, 3 * FT, FT), BF16),
            vmem((2, CC, 2 * FT, FT), BF16),
            vmem((2, CC, FT, FT), BF16),
            vmem((2, CC, NP, NUP, FT), BF16),
            vmem((CC, FT, FT), BF16),
            vmem((2 * CC, WT, LANES), BF16),
            vmem((2 * CC, WT, LANES), BF16),
            vmem((2 * CC, WT, LANES), BF16),
            vmem((2 * CC, WT, LANES), BF16),
            vmem((FT, CC * R), BF16),
            vmem((FT, CC * R), BF16),
            vmem((2, FT, CC * R), BF16),
            vmem((2, 3, FT, CC * R), BF16),
            vmem((2, CC, FT, FT), BF16),
            vmem((2, 2, CC, FT, FT), BF16),
            dma((4,)),
            dma((2, NP)),
            dma((CC,)),
            dma((2, 2, CC // CHUNK)),
            dma((2, 2, CC // CHUNK)),
            dma((2,)),
            dma((2, 3)),
            dma((2, 3)),
            dma((2, 2)),
            dma((2, 2)),
        ],
        compiler_params=pltpu.CompilerParams(
            collective_id=0, has_side_effects=True, vmem_limit_bytes=56 * 1024 * 1024
        ),
        name="sweeps",
    )(
        neighbours.T,
        jnp.asarray(selector(), BF16),
        right_sides,
        initial,
        inverse_blocks.transpose(0, 2, 1, 3),
        couplings.transpose(0, 2, 3, 1, 4),
    )


def solution(mesh):
    return jax.shard_map(
        functools.partial(local, mesh.shape["cross"]),
        mesh=mesh,
        in_specs=(
            P("sweep", "cross", None, None),
            P("sweep", "cross", None, None),
            P("sweep", "cross", None, None),
            P("sweep", "cross", None, None, None),
            P("cross", None),
        ),
        out_specs=P("sweep", "cross", None, None),
        check_vma=False,
    )
```

```python
import functools

import jax
import jax.numpy as jnp
import numpy as np
from jax import lax
from jax.experimental import pallas as pl
from jax.experimental.pallas import tpu as pltpu
from jax.sharding import PartitionSpec as P

MESH = pl.DeviceIdType.MESH
NU, NT, R, CC, NP = 135, 45, 32, 8, 4
FT = 48
LANES = NP * R
NUP = 144
F32, BF16 = jnp.float32, jnp.bfloat16
WT = 80
STACK = (1, 2, 3, 4, 5)
NSTACK = len(STACK) * FT
LOWER = 256
CHUNK = 2


def selector():
    rows = np.zeros((2 * WT + 3 * FT, NU), np.float32)
    for half, which in enumerate((2, 0)):
        others = [node for node in range(3) if node != which]
        for v in range(5):
            for a in range(3):
                for b in range(3):
                    rows[half * WT + 9 * v + 3 * a + b, 27 * v + 9 * a + 3 * b + which] = 1.0
                for place, c in enumerate(others):
                    slot = NT + 6 * v + 2 * a + place
                    rows[half * WT + slot, 27 * v + 9 * a + 3 * which + c] = 1.0
                    rows[2 * WT + FT * (1 + half) + 9 * v + 3 * a + c, slot] = 1.0
                slot = 9 * v + 3 * a + which
                rows[2 * WT + FT * (1 + half) + slot, slot] = 1.0
    for v in range(5):
        rows[2 * WT + 9 * v : 2 * WT + 9 * v + 9, 27 * v : 27 * v + 9] = np.eye(9)
    return rows


def nn(a, b):
    return lax.dot_general(a, b, (((1,), (0,)), ((), ())), preferred_element_type=F32)


def nt(a, b):
    return lax.dot_general(a, b, (((1,), (1,)), ((), ())), preferred_element_type=F32)


def blocks(rows):
    return lax.broadcasted_iota(jnp.int32, (rows, LANES), 1) // R


def by_block(rows, parts):
    block = blocks(rows)
    total = parts[0][1]
    for b, part in parts[1:]:
        total = jnp.where(block == b, part, total)
    return total


def kernel(
    crosses,
    neigh_hbm,
    sel_hbm,
    rhs_hbm,
    init_hbm,
    inv_hbm,
    cpl_hbm,
    out_hbm,
    neigh,
    sel,
    init_v,
    rhs_v,
    out_v,
    inv_n,
    cpl_n,
    turn_v,
    inv_v,
    stack_v,
    d_v,
    rows_v,
    w_v,
    x_v,
    v_v,
    t_v,
    us_v,
    q_v,
    face_v,
    col_v,
    u_v,
    w_face_v,
    l1_v,
    l2_v,
    l3_v,
    li_v,
    e_v,
    mm_v,
    ext_l0,
    ext_l1,
    ext_r0,
    ext_r1,
    up_s,
    up_r,
    a_s,
    a_r,
    m_s,
    m_r,
    load_sem,
    plane_sem,
    out_sem,
    halo_s,
    halo_r,
    upsem,
    a_ss,
    a_rs,
    m_ss,
    m_rs,
):
    ext_l, ext_r = (ext_l0, ext_l1), (ext_r0, ext_r1)
    s = lax.axis_index("sweep")
    k = lax.axis_index("cross")
    right = lax.rem(k + 1, crosses)
    left = lax.rem(k + crosses - 1, crosses)

    load_init = pltpu.make_async_copy(init_hbm, init_v, load_sem.at[0])
    load_rhs = pltpu.make_async_copy(rhs_hbm, rhs_v, load_sem.at[1])

    def inv_load(p):
        return pltpu.make_async_copy(inv_hbm.at[p], inv_n.at[p], plane_sem.at[0, p])

    def cpl_load(p):
        return pltpu.make_async_copy(cpl_hbm.at[p], cpl_n.at[p], plane_sem.at[1, p])

    load_sel = pltpu.make_async_copy(sel_hbm, sel, load_sem.at[2])
    load_neigh = pltpu.make_async_copy(neigh_hbm, neigh, load_sem.at[3])
    load_sel.start()
    load_init.start()
    for p in range(NP):
        inv_load(p).start()
        cpl_load(p).start()
    load_rhs.start()
    load_neigh.start()

    barrier = pltpu.get_barrier_semaphore()
    for other in (left, right):
        pl.semaphore_signal(barrier, inc=1, device_id={"cross": other}, device_id_type=MESH)
    for step in (1, 2, 3):
        pl.semaphore_signal(
            barrier, inc=1, device_id={"sweep": lax.rem(s + step, 4)}, device_id_type=MESH
        )

    def halo(sweep, part):
        def copy(ext, direction, first, to, other):
            return pltpu.make_async_remote_copy(
                ext.at[pl.ds(first + CHUNK * part, CHUNK)],
                ext.at[pl.ds(to + CHUNK * part, CHUNK)],
                halo_s.at[sweep, direction, part],
                halo_r.at[sweep, direction, part],
                device_id={"cross": other},
                device_id_type=MESH,
            )

        return (
            copy(ext_l[sweep], 0, CC, 0, right),
            copy(ext_r[sweep], 1, 0, CC, left),
        )

    up_copy = pltpu.make_async_remote_copy(
        up_s,
        up_r,
        upsem.at[0],
        upsem.at[1],
        device_id={"sweep": lax.rem(s + 3, 4)},
        device_id_type=MESH,
    )

    load_sel.wait()
    load_init.wait()
    up_s[...] = nt(sel[2 * WT : 2 * WT + FT], init_v[0].reshape(CC * R, NU)).astype(BF16)
    for c in range(CC):
        picked = nt(sel[0 : 2 * WT + FT, 0:NU], init_v[:, c].reshape(LANES, NU))
        ext_l[0][CC + c] = picked[0:WT].astype(BF16)
        ext_r[0][c] = picked[WT : 2 * WT].astype(BF16)
        us_v[c] = pltpu.roll(picked[2 * WT : 2 * WT + FT], LANES - R, 1)
        if c == CHUNK - 1:
            pl.semaphore_wait(barrier, 5)
        if c % CHUNK == CHUNK - 1:
            for copy in halo(0, c // CHUNK):
                copy.start()

    @pl.when(s > 0)
    def _():
        up_copy.start()

    def a_copy(sweep, step):
        to = lax.rem(s + step, 4) if sweep == 0 else lax.rem(s + 4 - step, 4)
        return pltpu.make_async_remote_copy(
            a_s.at[sweep],
            a_r.at[sweep, step - 1],
            a_ss.at[sweep, step - 1],
            a_rs.at[sweep, step - 1],
            device_id={"sweep": to},
            device_id_type=MESH,
        )

    def m_copy(sweep, step):
        to = lax.rem(s + step, 4) if sweep == 0 else lax.rem(s + 4 - step, 4)
        return pltpu.make_async_remote_copy(
            m_s.at[sweep],
            m_r.at[sweep, step - 1],
            m_ss.at[sweep, step - 1],
            m_rs.at[sweep, step - 1],
            device_id={"sweep": to},
            device_id_type=MESH,
        )

    def a_sends(sweep, step):
        return s + step < 4 if sweep == 0 else s >= step

    def a_takes(sweep, step):
        return s >= step if sweep == 0 else s + step < 4

    def m_sends(sweep, step):
        if sweep == 0:
            return jnp.logical_and(s >= 1, s + step < 4)
        return jnp.logical_and(s <= 2, s >= step)

    def m_takes(sweep, step):
        return s >= step + 1 if sweep == 0 else s + step <= 2

    @pl.when(s == 3)
    def _():
        up_r[...] = jnp.zeros_like(up_r)

    for step in (1, 2, 3):

        @pl.when(s < step)
        def _():
            a_r[0, step - 1] = jnp.zeros((FT, CC * R), BF16)

        @pl.when(s + step > 3)
        def _():
            a_r[1, step - 1] = jnp.zeros((FT, CC * R), BF16)

    for step in (1, 2):

        @pl.when(s < step + 1)
        def _():
            m_r[0, step - 1] = jnp.zeros((CC, FT, FT), BF16)

        @pl.when(s + step > 2)
        def _():
            m_r[1, step - 1] = jnp.zeros((CC, FT, FT), BF16)

    inv_v[:, :, NU - 7 : NUP] = jnp.zeros((CC, NP, NUP - NU + 7, NU), BF16)
    for place in list(range(len(STACK))) + [LOWER // FT]:
        top = LOWER if place == LOWER // FT else FT * place
        stack_v[:, :, top + 32 : top + FT] = jnp.zeros((CC, NP, 16, NU), BF16)
    stack_v[:, :, NSTACK:LOWER] = jnp.zeros((CC, NP, LOWER - NSTACK, NU), BF16)
    q_v[...] = jnp.zeros_like(q_v)
    for rows in (u_v, w_face_v):
        rows[:, 40:FT] = jnp.zeros((CC, FT - 40, LANES), F32)

    def turn(slot, block, count, to, p, first):
        flat = block.astype(F32).reshape(CC * count, NU)
        turn_v[0, slot, 0 : CC * count] = flat[:, 0:128]
        turn_v[1, slot, 0 : CC * count, 0 : NU - 128] = flat[:, 128:NU]
        for c in range(CC):
            rows = pl.ds(c, count, stride=CC)
            to[c, p, first : first + count, 0:128] = turn_v[0, slot, rows].astype(BF16)
            to[c, p, first : first + count, 128:NU] = turn_v[1, slot, rows][
                :, 0 : NU - 128
            ].astype(BF16)

    def turns(p):
        steps = []
        for first in range(0, NU, 16):
            steps.append((inv_n, (p,), inv_v, 0, first, min(16, NU - first)))
        for top, face in [(FT * place, face) for place, face in enumerate(STACK)] + [(LOWER, 0)]:
            for first in range(0, NT, 16):
                steps.append((cpl_n, (p, face), stack_v, top, first, min(16, NT - first)))
        return steps

    def product(p, c):
        d = nt(inv_v[c, p], stack_v[c, p])
        d_v[c, p] = d.astype(BF16)
        rows_v[c] = d[:, LOWER : LOWER + FT]
        for var in range(5):
            to = slice(9 * var, 9 * var + 9)
            q_v[c, p, to] = rows_v[c, 27 * var + 18 : 27 * var + 27]

    for p in range(NP):
        inv_load(p).wait()
        cpl_load(p).wait()
        for slot, (source, at, to, top, first, count) in enumerate(turns(p)):
            block = source[at + (slice(first, first + count),)]
            turn(slot, block, count, to, p, top + first)
            if p > 0 and slot % 3 == 0 and slot // 3 < CC:
                product(p - 1, slot // 3)
    for c in range(CC):
        product(NP - 1, c)
    load_rhs.wait()

    def by_plane(rows, stacked):
        return by_block(rows, [(p, stacked[rows * p : rows * p + rows]) for p in range(NP)])

    for c in range(CC):
        rhs = rhs_v[:, c].reshape(LANES, NU)
        w_v[c] = by_plane(NUP, nt(inv_v[c].reshape(NP * NUP, NU), rhs))

    def order_of(sweep):
        return list(range(NP)) if sweep == 0 else list(range(NP - 1, -1, -1))

    def d_in(sweep, c):
        low = LOWER if sweep == 0 else 0
        return d_v[c, :, :, low : low + FT]

    def sections(sweep):
        order = order_of(sweep)
        if sweep == 0:
            n = [[(-q_v[c, p]).astype(BF16) for p in order] for c in range(CC)]
        else:
            n = [[-face_v[c, p, :, 0:FT] for p in order] for c in range(CC)]
        two = [
            [nn(n[c][o], n[c][o - 1]).astype(BF16) for o in (1, 2, 3)] for c in range(CC)
        ]
        for c in range(CC):
            for o in (1, 2, 3):
                l1_v[sweep, c, FT * (o - 1) : FT * o] = n[c][o]
            for o in (2, 3):
                l2_v[sweep, c, FT * (o - 2) : FT * (o - 1)] = two[c][o - 1]
            li_v[c, 0] = n[c][0]
            li_v[c, 1] = two[c][0]
            l3_v[sweep, c] = nn(two[c][2], n[c][1]).astype(BF16)
            m_s[sweep, c] = nn(two[c][2], two[c][0]).astype(BF16)
        for step in (1, 2):

            @pl.when(m_sends(sweep, step))
            def _():
                m_copy(sweep, step).start()

    sections(0)

    def fronts_applied(sweep):
        order = order_of(sweep)
        for c in range(CC):
            first = li_v[c, 0]
            fronts = (first, li_v[c, 1], nn(l2_v[sweep, c, 0:FT], first).astype(BF16))
            e_v[sweep, c, order[0]] = d_in(sweep, c)[order[0]]
            for o in (1, 2, 3):
                e_v[sweep, c, order[o]] = nn(d_in(sweep, c)[order[o]], fronts[o - 1]).astype(BF16)

    def gathered(sweep, c, upper):
        low = lax.rem(neigh[2, c] - (k - 1) * CC + 2 * crosses * CC, crosses * CC)
        high = lax.rem(neigh[3, c] - k * CC + crosses * CC, crosses * CC)
        low = jnp.clip(low, 0, 2 * CC - 1)
        high = jnp.clip(high, 0, 2 * CC - 1)
        apart = [sel[2 * WT + FT * half : 2 * WT + FT * half + FT, 0:WT] for half in (1, 2)]
        col_v[c, 0:FT] = upper
        col_v[c, FT : 2 * FT] = nn(apart[0], ext_l[sweep][c]).astype(BF16)
        col_v[c, 2 * FT : 3 * FT] = nn(apart[1], ext_r[sweep][CC + c]).astype(BF16)
        col_v[c, 3 * FT : 4 * FT] = ext_l[sweep][low, 0:FT]
        col_v[c, 4 * FT : 5 * FT] = ext_r[sweep][high, 0:FT]

    def shift_of(sweep, steps):
        return R * steps if sweep == 0 else LANES - R * steps

    def applied_to_column(c):
        d = d_v[c].reshape(NP * NUP, LOWER + FT)[:, 0:NSTACK]
        return by_plane(NUP, nn(d, col_v[c]))

    def local_faces(sweep):
        order = order_of(sweep)
        block = blocks(FT)
        for c in range(CC):
            total = u_v[c]
            for steps, left_v in ((1, l1_v), (2, l2_v), (3, l3_v)):
                moved = pltpu.roll(u_v[c], shift_of(sweep, steps), 1).astype(BF16)
                z = nn(left_v[sweep, c], moved)
                for o in range(steps, NP):
                    part = z[FT * (o - steps) : FT * (o - steps + 1)]
                    total = total + jnp.where(block == order[o], part, 0.0)
            t_v[c] = total
        for g in range(2):
            total = jnp.zeros((FT, LANES), F32)
            for b in range(4):
                total = packed(sweep, b, t_v[4 * g + b], total)
            a_s[sweep, :, LANES * g : LANES * g + LANES] = total.astype(BF16)

    def before_of(sweep, c):
        moved = pltpu.roll(t_v[c], shift_of(sweep, 1), 1)
        return jnp.where(blocks(FT) == order_of(sweep)[0], 0.0, moved).astype(BF16)

    def packed(sweep, b, now, total):
        last = 3 if sweep == 0 else 0
        turned_in = now if b == last else pltpu.roll(now, (R * (b - last)) % LANES, 1)
        return jnp.where(blocks(FT) == b, turned_in, total)

    def spread(b, group):
        one = jnp.where(blocks(FT) == b, group, 0.0)
        one = one + pltpu.roll(one, R, 1)
        return one + pltpu.roll(one, 2 * R, 1)

    def send_ends(sweep):
        for step in (1, 2, 3):

            @pl.when(a_sends(sweep, step))
            def _():
                a_copy(sweep, step).start()

    def take_operators(sweep):
        for step in (1, 2):

            @pl.when(m_takes(sweep, step))
            def _():
                m_copy(sweep, step).wait_recv()

        for c in range(CC):
            mm_v[c] = nn(m_r[sweep, 0, c], m_r[sweep, 1, c]).astype(BF16)

    def take_ends(sweep):
        for step in (1, 2, 3):

            @pl.when(a_takes(sweep, step))
            def _():
                a_copy(sweep, step).wait_recv()

    def incoming(sweep, g):
        lanes = slice(LANES * g, LANES * g + LANES)
        parts = []
        for b in range(4):
            c = 4 * g + b
            one = nn(m_r[sweep, 0, c], a_r[sweep, 1, :, lanes])
            parts.append((b, one + nn(mm_v[c], a_r[sweep, 2, :, lanes])))
        return a_r[sweep, 0, :, lanes].astype(F32) + by_block(FT, parts)

    def corrected(sweep, c, b, entering):
        t = spread(b, entering).astype(BF16)
        return v_v[c] - by_plane(NUP, nn(e_v[sweep, c].reshape(NP * NUP, FT), t))

    load_neigh.wait()
    for part in range(CC // CHUNK):
        for copy in halo(0, part):
            copy.wait_recv()

    @pl.when(s < 3)
    def _():
        up_copy.wait_recv()

    for c in range(CC):
        g, b = c // 4, c % 4
        edge = up_r[:, LANES * g : LANES * g + LANES].astype(F32)
        edge = pltpu.roll(edge, (R * (3 - b)) % LANES, 1) if b != 3 else edge
        gathered(0, c, jnp.where(blocks(FT) == 3, edge, us_v[c]).astype(BF16))
    for c in range(CC):
        x = applied_to_column(c)
        x_v[c] = x
        v_v[c] = w_v[c] - x
        for var in range(5):
            u_v[c, 9 * var : 9 * var + 9] = v_v[c, 27 * var + 18 : 27 * var + 27]
    local_faces(0)
    send_ends(0)
    fronts_applied(0)
    for c in range(CC):
        y = nn(d_in(0, c).reshape(NP * NUP, FT), before_of(0, c))
        v_v[c] = v_v[c] - by_plane(NUP, y)
    take_operators(0)
    take_ends(0)
    for g in range(2):
        entering = incoming(0, g)
        for b in range(4):
            c = 4 * g + b
            middle = corrected(0, c, b, entering)
            picked = nn(sel[0 : 2 * WT, 0:NU], middle[0:NU].astype(BF16)).astype(BF16)
            ext_l[1][CC + c] = picked[0:WT]
            ext_r[1][c] = picked[WT : 2 * WT]
            if c % CHUNK == CHUNK - 1:
                for copy in halo(1, c // CHUNK):
                    copy.start()
            w_v[c] = middle + x_v[c]
    for c in range(CC):
        for p in range(NP):
            face_v[c, p] = nn(sel[2 * WT : 2 * WT + FT], d_v[c, p, 0:NU, 0:NSTACK]).astype(BF16)
        for var in range(5):
            w_face_v[c, 9 * var : 9 * var + 9] = w_v[c, 27 * var : 27 * var + 9]
    sections(1)
    fronts_applied(1)

    for part in range(CC // CHUNK):
        for copy in halo(1, part):
            copy.wait_recv()
    for c in range(CC):
        gathered(1, c, jnp.zeros((FT, LANES), BF16))
    for c in range(CC):
        faces = face_v[c].reshape(NP * FT, NSTACK)
        u_v[c] = w_face_v[c] - by_plane(FT, nn(faces, col_v[c]))
    local_faces(1)
    send_ends(1)
    for c in range(CC):
        col_v[c, 0:FT] = before_of(1, c)
    for c in range(CC):
        v_v[c] = w_v[c] - applied_to_column(c)
    take_operators(1)
    take_ends(1)

    def out_store(c):
        return pltpu.make_async_copy(out_v.at[:, c], out_hbm.at[:, c], out_sem.at[c])

    same = (
        lax.broadcasted_iota(jnp.int32, (LANES, LANES), 0)
        == lax.broadcasted_iota(jnp.int32, (LANES, LANES), 1)
    ).astype(BF16)
    for g in range(2):
        entering = incoming(1, g)
        for b in range(4):
            c = 4 * g + b
            result = corrected(1, c, b, entering)[0:NU].astype(BF16)
            out_v[:, c] = nt(same, result).astype(BF16).reshape(NP, R, NU)
            out_store(c).start()
    for c in range(CC):
        out_store(c).wait()

    for sweep in (0, 1):
        for part in range(CC // CHUNK):
            for copy in halo(sweep, part):
                copy.wait_send()
        for step in (1, 2, 3):

            @pl.when(a_sends(sweep, step))
            def _():
                a_copy(sweep, step).wait_send()

        for step in (1, 2):

            @pl.when(m_sends(sweep, step))
            def _():
                m_copy(sweep, step).wait_send()

    @pl.when(s > 0)
    def _():
        up_copy.wait_send()


def local(crosses, right_sides, initial, inverse_blocks, couplings, neighbours):
    hbm = pl.BlockSpec(memory_space=pltpu.HBM)
    vmem = pltpu.VMEM
    dma = pltpu.SemaphoreType.DMA
    return pl.pallas_call(
        functools.partial(kernel, crosses),
        out_shape=jax.ShapeDtypeStruct(right_sides.shape, BF16),
        in_specs=[
            hbm,
            hbm,
            hbm,
            hbm,
            hbm,
            hbm,
        ],
        out_specs=pl.BlockSpec(memory_space=pl.ANY),
        scratch_shapes=[
            pltpu.SMEM((4, CC), jnp.int32),
            vmem((2 * WT + 3 * FT, NU), BF16),
            vmem((NP, CC, R, NU), BF16),
            vmem((NP, CC, R, NU), BF16),
            vmem((NP, CC, R, NU), BF16),
            vmem((NP, NU, CC, NU), BF16),
            vmem((NP, 6, NT, CC, NU), BF16),
            vmem((2, 27, 16 * CC, 128), F32),
            vmem((CC, NP, NUP, NU), BF16),
            vmem((CC, NP, LOWER + FT, NU), BF16),
            vmem((CC, NP, NUP, LOWER + FT), BF16),
            vmem((CC, NUP, FT), F32),
            vmem((CC, NUP, LANES), F32),
            vmem((CC, NUP, LANES), F32),
            vmem((CC, NUP, LANES), F32),
            vmem((CC, FT, LANES), F32),
            vmem((CC, FT, LANES), F32),
            vmem((CC, NP, FT, FT), F32),
            vmem((CC, NP, FT, NSTACK), BF16),
            vmem((CC, NSTACK, LANES), BF16),
            vmem((CC, FT, LANES), F32),
            vmem((CC, FT, LANES), F32),
            vmem((2, CC, 3 * FT, FT), BF16),
            vmem((2, CC, 2 * FT, FT), BF16),
            vmem((2, CC, FT, FT), BF16),
            vmem((CC, 2, FT, FT), BF16),
            vmem((2, CC, NP, NUP, FT), BF16),
            vmem((CC, FT, FT), BF16),
            vmem((2 * CC, WT, LANES), BF16),
            vmem((2 * CC, WT, LANES), BF16),
            vmem((2 * CC, WT, LANES), BF16),
            vmem((2 * CC, WT, LANES), BF16),
            vmem((FT, CC * R), BF16),
            vmem((FT, CC * R), BF16),
            vmem((2, FT, CC * R), BF16),
            vmem((2, 3, FT, CC * R), BF16),
            vmem((2, CC, FT, FT), BF16),
            vmem((2, 2, CC, FT, FT), BF16),
            dma((4,)),
            dma((2, NP)),
            dma((CC,)),
            dma((2, 2, CC // CHUNK)),
            dma((2, 2, CC // CHUNK)),
            dma((2,)),
            dma((2, 3)),
            dma((2, 3)),
            dma((2, 2)),
            dma((2, 2)),
        ],
        compiler_params=pltpu.CompilerParams(
            collective_id=0, has_side_effects=True, vmem_limit_bytes=56 * 1024 * 1024
        ),
        name="sweeps",
    )(
        neighbours.T,
        jnp.asarray(selector(), BF16),
        right_sides,
        initial,
        inverse_blocks.transpose(0, 2, 1, 3),
        couplings.transpose(0, 2, 3, 1, 4),
    )


def solution(mesh):
    return jax.shard_map(
        functools.partial(local, mesh.shape["cross"]),
        mesh=mesh,
        in_specs=(
            P("sweep", "cross", None, None),
            P("sweep", "cross", None, None),
            P("sweep", "cross", None, None),
            P("sweep", "cross", None, None, None),
            P("cross", None),
        ),
        out_specs=P("sweep", "cross", None, None),
        check_vma=False,
    )
```

```python
import functools

import jax
import jax.numpy as jnp
import numpy as np
from jax import lax
from jax.experimental import pallas as pl
from jax.experimental.pallas import tpu as pltpu
from jax.sharding import PartitionSpec as P

MESH = pl.DeviceIdType.MESH
NU, NT, R, CC, NP = 135, 45, 32, 8, 4
FT = 48
LANES = NP * R
NUP = 144
F32, BF16 = jnp.float32, jnp.bfloat16
WT = 80
STACK = (1, 2, 3, 4, 5)
NSTACK = len(STACK) * FT
LOWER = 256
CHUNK = 2


def selector():
    rows = np.zeros((2 * WT + 3 * FT, NU), np.float32)
    for half, which in enumerate((2, 0)):
        others = [node for node in range(3) if node != which]
        for v in range(5):
            for a in range(3):
                for b in range(3):
                    rows[half * WT + 9 * v + 3 * a + b, 27 * v + 9 * a + 3 * b + which] = 1.0
                for place, c in enumerate(others):
                    slot = NT + 6 * v + 2 * a + place
                    rows[half * WT + slot, 27 * v + 9 * a + 3 * which + c] = 1.0
                    rows[2 * WT + FT * (1 + half) + 9 * v + 3 * a + c, slot] = 1.0
                slot = 9 * v + 3 * a + which
                rows[2 * WT + FT * (1 + half) + slot, slot] = 1.0
    for v in range(5):
        rows[2 * WT + 9 * v : 2 * WT + 9 * v + 9, 27 * v : 27 * v + 9] = np.eye(9)
    return rows


def nn(a, b):
    return lax.dot_general(a, b, (((1,), (0,)), ((), ())), preferred_element_type=F32)


def nt(a, b):
    return lax.dot_general(a, b, (((1,), (1,)), ((), ())), preferred_element_type=F32)


def blocks(rows):
    return lax.broadcasted_iota(jnp.int32, (rows, LANES), 1) // R


def by_block(rows, parts):
    block = blocks(rows)
    total = parts[0][1]
    for b, part in parts[1:]:
        total = jnp.where(block == b, part, total)
    return total


def kernel(
    crosses,
    neigh_hbm,
    sel_hbm,
    rhs_hbm,
    init_hbm,
    inv_hbm,
    cpl_hbm,
    out_hbm,
    neigh,
    sel,
    init_v,
    rhs_v,
    out_v,
    inv_n,
    cpl_n,
    turn_v,
    inv_v,
    stack_v,
    d_v,
    rows_v,
    w_v,
    x_v,
    v_v,
    t_v,
    us_v,
    q_v,
    face_v,
    col_v,
    u_v,
    w_face_v,
    l1_v,
    l2_v,
    l3_v,
    li_v,
    e_v,
    mm_v,
    ext_l0,
    ext_l1,
    ext_r0,
    ext_r1,
    up_s,
    up_r,
    a_s,
    a_r,
    m_s,
    m_r,
    load_sem,
    plane_sem,
    out_sem,
    halo_s,
    halo_r,
    upsem,
    a_ss,
    a_rs,
    m_ss,
    m_rs,
):
    ext_l, ext_r = (ext_l0, ext_l1), (ext_r0, ext_r1)
    s = lax.axis_index("sweep")
    k = lax.axis_index("cross")
    right = lax.rem(k + 1, crosses)
    left = lax.rem(k + crosses - 1, crosses)

    load_init = pltpu.make_async_copy(init_hbm, init_v, load_sem.at[0])
    load_rhs = pltpu.make_async_copy(rhs_hbm, rhs_v, load_sem.at[1])

    def inv_load(p):
        return pltpu.make_async_copy(inv_hbm.at[p], inv_n.at[p], plane_sem.at[0, p])

    def cpl_load(p):
        return pltpu.make_async_copy(cpl_hbm.at[p], cpl_n.at[p], plane_sem.at[1, p])

    load_sel = pltpu.make_async_copy(sel_hbm, sel, load_sem.at[2])
    load_neigh = pltpu.make_async_copy(neigh_hbm, neigh, load_sem.at[3])
    load_sel.start()
    load_init.start()
    for p in range(NP):
        inv_load(p).start()
        cpl_load(p).start()
    load_rhs.start()
    load_neigh.start()

    barrier = pltpu.get_barrier_semaphore()
    for other in (left, right):
        pl.semaphore_signal(barrier, inc=1, device_id={"cross": other}, device_id_type=MESH)
    for step in (1, 2, 3):
        pl.semaphore_signal(
            barrier, inc=1, device_id={"sweep": lax.rem(s + step, 4)}, device_id_type=MESH
        )

    def halo(sweep, part):
        def copy(ext, direction, first, to, other):
            return pltpu.make_async_remote_copy(
                ext.at[pl.ds(first + CHUNK * part, CHUNK)],
                ext.at[pl.ds(to + CHUNK * part, CHUNK)],
                halo_s.at[sweep, direction, part],
                halo_r.at[sweep, direction, part],
                device_id={"cross": other},
                device_id_type=MESH,
            )

        return (
            copy(ext_l[sweep], 0, CC, 0, right),
            copy(ext_r[sweep], 1, 0, CC, left),
        )

    up_copy = pltpu.make_async_remote_copy(
        up_s,
        up_r,
        upsem.at[0],
        upsem.at[1],
        device_id={"sweep": lax.rem(s + 3, 4)},
        device_id_type=MESH,
    )

    load_sel.wait()
    load_init.wait()
    up_s[...] = nt(sel[2 * WT : 2 * WT + FT], init_v[0].reshape(CC * R, NU)).astype(BF16)
    for c in range(CC):
        picked = nt(sel[0 : 2 * WT + FT, 0:NU], init_v[:, c].reshape(LANES, NU))
        ext_l[0][CC + c] = picked[0:WT].astype(BF16)
        ext_r[0][c] = picked[WT : 2 * WT].astype(BF16)
        us_v[c] = pltpu.roll(picked[2 * WT : 2 * WT + FT], LANES - R, 1)
        if c == CHUNK - 1:
            pl.semaphore_wait(barrier, 5)
        if c % CHUNK == CHUNK - 1:
            for copy in halo(0, c // CHUNK):
                copy.start()

    @pl.when(s > 0)
    def _():
        up_copy.start()

    def a_copy(sweep, step):
        to = lax.rem(s + step, 4) if sweep == 0 else lax.rem(s + 4 - step, 4)
        return pltpu.make_async_remote_copy(
            a_s.at[sweep],
            a_r.at[sweep, step - 1],
            a_ss.at[sweep, step - 1],
            a_rs.at[sweep, step - 1],
            device_id={"sweep": to},
            device_id_type=MESH,
        )

    def m_copy(sweep, step):
        to = lax.rem(s + step, 4) if sweep == 0 else lax.rem(s + 4 - step, 4)
        return pltpu.make_async_remote_copy(
            m_s.at[sweep],
            m_r.at[sweep, step - 1],
            m_ss.at[sweep, step - 1],
            m_rs.at[sweep, step - 1],
            device_id={"sweep": to},
            device_id_type=MESH,
        )

    def a_sends(sweep, step):
        return s + step < 4 if sweep == 0 else s >= step

    def a_takes(sweep, step):
        return s >= step if sweep == 0 else s + step < 4

    def m_sends(sweep, step):
        if sweep == 0:
            return jnp.logical_and(s >= 1, s + step < 4)
        return jnp.logical_and(s <= 2, s >= step)

    def m_takes(sweep, step):
        return s >= step + 1 if sweep == 0 else s + step <= 2

    @pl.when(s == 3)
    def _():
        up_r[...] = jnp.zeros_like(up_r)

    for step in (1, 2, 3):

        @pl.when(s < step)
        def _():
            a_r[0, step - 1] = jnp.zeros((FT, CC * R), BF16)

        @pl.when(s + step > 3)
        def _():
            a_r[1, step - 1] = jnp.zeros((FT, CC * R), BF16)

    for step in (1, 2):

        @pl.when(s < step + 1)
        def _():
            m_r[0, step - 1] = jnp.zeros((CC, FT, FT), BF16)

        @pl.when(s + step > 2)
        def _():
            m_r[1, step - 1] = jnp.zeros((CC, FT, FT), BF16)

    inv_v[:, :, NU - 7 : NUP] = jnp.zeros((CC, NP, NUP - NU + 7, NU), BF16)
    for place in list(range(len(STACK))) + [LOWER // FT]:
        top = LOWER if place == LOWER // FT else FT * place
        stack_v[:, :, top + 32 : top + FT] = jnp.zeros((CC, NP, 16, NU), BF16)
    stack_v[:, :, NSTACK:LOWER] = jnp.zeros((CC, NP, LOWER - NSTACK, NU), BF16)
    q_v[...] = jnp.zeros_like(q_v)
    for rows in (u_v, w_face_v):
        rows[:, 40:FT] = jnp.zeros((CC, FT - 40, LANES), F32)

    def turn(slot, block, count, to, p, first):
        flat = block.astype(F32).reshape(CC * count, NU)
        turn_v[0, slot, 0 : CC * count] = flat[:, 0:128]
        turn_v[1, slot, 0 : CC * count, 0 : NU - 128] = flat[:, 128:NU]
        for c in range(CC):
            rows = pl.ds(c, count, stride=CC)
            to[c, p, first : first + count, 0:128] = turn_v[0, slot, rows].astype(BF16)
            to[c, p, first : first + count, 128:NU] = turn_v[1, slot, rows][
                :, 0 : NU - 128
            ].astype(BF16)

    def products(p, carry):
        inv_load(p).wait()
        cpl_load(p).wait()
        slot = 0
        for first in range(0, NU, 16):
            count = min(16, NU - first)
            turn(slot, inv_n[p, first : first + count], count, inv_v, p, first)
            slot += 1
        for top, face in [(FT * place, face) for place, face in enumerate(STACK)] + [(LOWER, 0)]:
            for first in range(0, NT, 16):
                count = min(16, NT - first)
                block = cpl_n[p, face, first : first + count]
                turn(slot, block, count, stack_v, p, top + first)
                slot += 1
        for c in range(CC):
            d = nt(inv_v[c, p], stack_v[c, p])
            d_v[c, p] = d.astype(BF16)
            rows_v[c] = d[:, LOWER : LOWER + FT]
            for var in range(5):
                to = slice(9 * var, 9 * var + 9)
                q_v[c, p, to] = rows_v[c, 27 * var + 18 : 27 * var + 27]
        return carry

    lax.fori_loop(0, NP, products, 0)
    load_rhs.wait()

    def by_plane(rows, stacked):
        return by_block(rows, [(p, stacked[rows * p : rows * p + rows]) for p in range(NP)])

    for c in range(CC):
        rhs = rhs_v[:, c].reshape(LANES, NU)
        w_v[c] = by_plane(NUP, nt(inv_v[c].reshape(NP * NUP, NU), rhs))

    def order_of(sweep):
        return list(range(NP)) if sweep == 0 else list(range(NP - 1, -1, -1))

    def d_in(sweep, c):
        low = LOWER if sweep == 0 else 0
        return d_v[c, :, :, low : low + FT]

    def sections(sweep):
        order = order_of(sweep)
        if sweep == 0:
            n = [[(-q_v[c, p]).astype(BF16) for p in order] for c in range(CC)]
        else:
            n = [[-face_v[c, p, :, 0:FT] for p in order] for c in range(CC)]
        two = [
            [nn(n[c][o], n[c][o - 1]).astype(BF16) for o in (1, 2, 3)] for c in range(CC)
        ]
        for c in range(CC):
            for o in (1, 2, 3):
                l1_v[sweep, c, FT * (o - 1) : FT * o] = n[c][o]
            for o in (2, 3):
                l2_v[sweep, c, FT * (o - 2) : FT * (o - 1)] = two[c][o - 1]
            li_v[c, 0] = n[c][0]
            li_v[c, 1] = two[c][0]
            l3_v[sweep, c] = nn(two[c][2], n[c][1]).astype(BF16)
            m_s[sweep, c] = nn(two[c][2], two[c][0]).astype(BF16)
        for step in (1, 2):

            @pl.when(m_sends(sweep, step))
            def _():
                m_copy(sweep, step).start()

    sections(0)

    def fronts_applied(sweep):
        order = order_of(sweep)
        for c in range(CC):
            first = li_v[c, 0]
            fronts = (first, li_v[c, 1], nn(l2_v[sweep, c, 0:FT], first).astype(BF16))
            e_v[sweep, c, order[0]] = d_in(sweep, c)[order[0]]
            for o in (1, 2, 3):
                e_v[sweep, c, order[o]] = nn(d_in(sweep, c)[order[o]], fronts[o - 1]).astype(BF16)

    def gathered(sweep, c, upper):
        low = lax.rem(neigh[2, c] - (k - 1) * CC + 2 * crosses * CC, crosses * CC)
        high = lax.rem(neigh[3, c] - k * CC + crosses * CC, crosses * CC)
        low = jnp.clip(low, 0, 2 * CC - 1)
        high = jnp.clip(high, 0, 2 * CC - 1)
        apart = [sel[2 * WT + FT * half : 2 * WT + FT * half + FT, 0:WT] for half in (1, 2)]
        col_v[c, 0:FT] = upper
        col_v[c, FT : 2 * FT] = nn(apart[0], ext_l[sweep][c]).astype(BF16)
        col_v[c, 2 * FT : 3 * FT] = nn(apart[1], ext_r[sweep][CC + c]).astype(BF16)
        col_v[c, 3 * FT : 4 * FT] = ext_l[sweep][low, 0:FT]
        col_v[c, 4 * FT : 5 * FT] = ext_r[sweep][high, 0:FT]

    def shift_of(sweep, steps):
        return R * steps if sweep == 0 else LANES - R * steps

    def applied_to_column(c):
        d = d_v[c].reshape(NP * NUP, LOWER + FT)[:, 0:NSTACK]
        return by_plane(NUP, nn(d, col_v[c]))

    def local_faces(sweep):
        order = order_of(sweep)
        block = blocks(FT)
        for c in range(CC):
            total = u_v[c]
            for steps, left_v in ((1, l1_v), (2, l2_v), (3, l3_v)):
                moved = pltpu.roll(u_v[c], shift_of(sweep, steps), 1).astype(BF16)
                z = nn(left_v[sweep, c], moved)
                for o in range(steps, NP):
                    part = z[FT * (o - steps) : FT * (o - steps + 1)]
                    total = total + jnp.where(block == order[o], part, 0.0)
            t_v[c] = total
        for g in range(2):
            total = jnp.zeros((FT, LANES), F32)
            for b in range(4):
                total = packed(sweep, b, t_v[4 * g + b], total)
            a_s[sweep, :, LANES * g : LANES * g + LANES] = total.astype(BF16)

    def before_of(sweep, c):
        moved = pltpu.roll(t_v[c], shift_of(sweep, 1), 1)
        return jnp.where(blocks(FT) == order_of(sweep)[0], 0.0, moved).astype(BF16)

    def packed(sweep, b, now, total):
        last = 3 if sweep == 0 else 0
        turned_in = now if b == last else pltpu.roll(now, (R * (b - last)) % LANES, 1)
        return jnp.where(blocks(FT) == b, turned_in, total)

    def spread(b, group):
        one = jnp.where(blocks(FT) == b, group, 0.0)
        one = one + pltpu.roll(one, R, 1)
        return one + pltpu.roll(one, 2 * R, 1)

    def send_ends(sweep):
        for step in (1, 2, 3):

            @pl.when(a_sends(sweep, step))
            def _():
                a_copy(sweep, step).start()

    def take_operators(sweep):
        for step in (1, 2):

            @pl.when(m_takes(sweep, step))
            def _():
                m_copy(sweep, step).wait_recv()

        for c in range(CC):
            mm_v[c] = nn(m_r[sweep, 0, c], m_r[sweep, 1, c]).astype(BF16)

    def take_ends(sweep):
        for step in (1, 2, 3):

            @pl.when(a_takes(sweep, step))
            def _():
                a_copy(sweep, step).wait_recv()

    def incoming(sweep, g):
        lanes = slice(LANES * g, LANES * g + LANES)
        parts = []
        for b in range(4):
            c = 4 * g + b
            one = nn(m_r[sweep, 0, c], a_r[sweep, 1, :, lanes])
            parts.append((b, one + nn(mm_v[c], a_r[sweep, 2, :, lanes])))
        return a_r[sweep, 0, :, lanes].astype(F32) + by_block(FT, parts)

    def corrected(sweep, c, b, entering):
        t = spread(b, entering).astype(BF16)
        return v_v[c] - by_plane(NUP, nn(e_v[sweep, c].reshape(NP * NUP, FT), t))

    load_neigh.wait()
    for part in range(CC // CHUNK):
        for copy in halo(0, part):
            copy.wait_recv()

    @pl.when(s < 3)
    def _():
        up_copy.wait_recv()

    for c in range(CC):
        g, b = c // 4, c % 4
        edge = up_r[:, LANES * g : LANES * g + LANES].astype(F32)
        edge = pltpu.roll(edge, (R * (3 - b)) % LANES, 1) if b != 3 else edge
        gathered(0, c, jnp.where(blocks(FT) == 3, edge, us_v[c]).astype(BF16))
    for c in range(CC):
        x = applied_to_column(c)
        x_v[c] = x
        v_v[c] = w_v[c] - x
        for var in range(5):
            u_v[c, 9 * var : 9 * var + 9] = v_v[c, 27 * var + 18 : 27 * var + 27]
    local_faces(0)
    send_ends(0)
    fronts_applied(0)
    for c in range(CC):
        y = nn(d_in(0, c).reshape(NP * NUP, FT), before_of(0, c))
        v_v[c] = v_v[c] - by_plane(NUP, y)
    take_operators(0)
    take_ends(0)
    for g in range(2):
        entering = incoming(0, g)
        for b in range(4):
            c = 4 * g + b
            middle = corrected(0, c, b, entering)
            picked = nn(sel[0 : 2 * WT, 0:NU], middle[0:NU].astype(BF16)).astype(BF16)
            ext_l[1][CC + c] = picked[0:WT]
            ext_r[1][c] = picked[WT : 2 * WT]
            if c % CHUNK == CHUNK - 1:
                for copy in halo(1, c // CHUNK):
                    copy.start()
            w_v[c] = middle + x_v[c]
    for c in range(CC):
        for p in range(NP):
            face_v[c, p] = nn(sel[2 * WT : 2 * WT + FT], d_v[c, p, 0:NU, 0:NSTACK]).astype(BF16)
        for var in range(5):
            w_face_v[c, 9 * var : 9 * var + 9] = w_v[c, 27 * var : 27 * var + 9]
    sections(1)
    fronts_applied(1)

    for part in range(CC // CHUNK):
        for copy in halo(1, part):
            copy.wait_recv()
    for c in range(CC):
        gathered(1, c, jnp.zeros((FT, LANES), BF16))
    for c in range(CC):
        faces = face_v[c].reshape(NP * FT, NSTACK)
        u_v[c] = w_face_v[c] - by_plane(FT, nn(faces, col_v[c]))
    local_faces(1)
    send_ends(1)
    for c in range(CC):
        col_v[c, 0:FT] = before_of(1, c)
    for c in range(CC):
        v_v[c] = w_v[c] - applied_to_column(c)
    take_operators(1)
    take_ends(1)

    def out_store(c):
        return pltpu.make_async_copy(out_v.at[:, c], out_hbm.at[:, c], out_sem.at[c])

    same = (
        lax.broadcasted_iota(jnp.int32, (LANES, LANES), 0)
        == lax.broadcasted_iota(jnp.int32, (LANES, LANES), 1)
    ).astype(BF16)
    for g in range(2):
        entering = incoming(1, g)
        for b in range(4):
            c = 4 * g + b
            result = corrected(1, c, b, entering)[0:NU].astype(BF16)
            out_v[:, c] = nt(same, result).astype(BF16).reshape(NP, R, NU)
            out_store(c).start()
    for c in range(CC):
        out_store(c).wait()

    for sweep in (0, 1):
        for part in range(CC // CHUNK):
            for copy in halo(sweep, part):
                copy.wait_send()
        for step in (1, 2, 3):

            @pl.when(a_sends(sweep, step))
            def _():
                a_copy(sweep, step).wait_send()

        for step in (1, 2):

            @pl.when(m_sends(sweep, step))
            def _():
                m_copy(sweep, step).wait_send()

    @pl.when(s > 0)
    def _():
        up_copy.wait_send()


def local(crosses, right_sides, initial, inverse_blocks, couplings, neighbours):
    hbm = pl.BlockSpec(memory_space=pltpu.HBM)
    vmem = pltpu.VMEM
    dma = pltpu.SemaphoreType.DMA
    return pl.pallas_call(
        functools.partial(kernel, crosses),
        out_shape=jax.ShapeDtypeStruct(right_sides.shape, BF16),
        in_specs=[
            hbm,
            hbm,
            hbm,
            hbm,
            hbm,
            hbm,
        ],
        out_specs=pl.BlockSpec(memory_space=pl.ANY),
        scratch_shapes=[
            pltpu.SMEM((4, CC), jnp.int32),
            vmem((2 * WT + 3 * FT, NU), BF16),
            vmem((NP, CC, R, NU), BF16),
            vmem((NP, CC, R, NU), BF16),
            vmem((NP, CC, R, NU), BF16),
            vmem((NP, NU, CC, NU), BF16),
            vmem((NP, 6, NT, CC, NU), BF16),
            vmem((2, 27, 16 * CC, 128), F32),
            vmem((CC, NP, NUP, NU), BF16),
            vmem((CC, NP, LOWER + FT, NU), BF16),
            vmem((CC, NP, NUP, LOWER + FT), BF16),
            vmem((CC, NUP, FT), F32),
            vmem((CC, NUP, LANES), F32),
            vmem((CC, NUP, LANES), F32),
            vmem((CC, NUP, LANES), F32),
            vmem((CC, FT, LANES), F32),
            vmem((CC, FT, LANES), F32),
            vmem((CC, NP, FT, FT), F32),
            vmem((CC, NP, FT, NSTACK), BF16),
            vmem((CC, NSTACK, LANES), BF16),
            vmem((CC, FT, LANES), F32),
            vmem((CC, FT, LANES), F32),
            vmem((2, CC, 3 * FT, FT), BF16),
            vmem((2, CC, 2 * FT, FT), BF16),
            vmem((2, CC, FT, FT), BF16),
            vmem((CC, 2, FT, FT), BF16),
            vmem((2, CC, NP, NUP, FT), BF16),
            vmem((CC, FT, FT), BF16),
            vmem((2 * CC, WT, LANES), BF16),
            vmem((2 * CC, WT, LANES), BF16),
            vmem((2 * CC, WT, LANES), BF16),
            vmem((2 * CC, WT, LANES), BF16),
            vmem((FT, CC * R), BF16),
            vmem((FT, CC * R), BF16),
            vmem((2, FT, CC * R), BF16),
            vmem((2, 3, FT, CC * R), BF16),
            vmem((2, CC, FT, FT), BF16),
            vmem((2, 2, CC, FT, FT), BF16),
            dma((4,)),
            dma((2, NP)),
            dma((CC,)),
            dma((2, 2, CC // CHUNK)),
            dma((2, 2, CC // CHUNK)),
            dma((2,)),
            dma((2, 3)),
            dma((2, 3)),
            dma((2, 2)),
            dma((2, 2)),
        ],
        compiler_params=pltpu.CompilerParams(
            collective_id=0, has_side_effects=True, vmem_limit_bytes=56 * 1024 * 1024
        ),
        name="sweeps",
    )(
        neighbours.T,
        jnp.asarray(selector(), BF16),
        right_sides,
        initial,
        inverse_blocks.transpose(0, 2, 1, 3),
        couplings.transpose(0, 2, 3, 1, 4),
    )


def solution(mesh):
    return jax.shard_map(
        functools.partial(local, mesh.shape["cross"]),
        mesh=mesh,
        in_specs=(
            P("sweep", "cross", None, None),
            P("sweep", "cross", None, None),
            P("sweep", "cross", None, None),
            P("sweep", "cross", None, None, None),
            P("cross", None),
        ),
        out_specs=P("sweep", "cross", None, None),
        check_vma=False,
    )
```

```python
import functools

import jax
import jax.numpy as jnp
import numpy as np
from jax import lax
from jax.experimental import pallas as pl
from jax.experimental.pallas import tpu as pltpu
from jax.sharding import PartitionSpec as P

MESH = pl.DeviceIdType.MESH
NU, NT, R, CC, NP = 135, 45, 32, 8, 4
FT = 48
LANES = NP * R
NUP = 144
F32, BF16 = jnp.float32, jnp.bfloat16
WT = 80
STACK = (1, 2, 3, 4, 5)
NSTACK = len(STACK) * FT
LOWER = 256
CHUNK = 1


def selector():
    rows = np.zeros((2 * WT + 3 * FT, NU), np.float32)
    for half, which in enumerate((2, 0)):
        others = [node for node in range(3) if node != which]
        for v in range(5):
            for a in range(3):
                for b in range(3):
                    rows[half * WT + 9 * v + 3 * a + b, 27 * v + 9 * a + 3 * b + which] = 1.0
                for place, c in enumerate(others):
                    slot = NT + 6 * v + 2 * a + place
                    rows[half * WT + slot, 27 * v + 9 * a + 3 * which + c] = 1.0
                    rows[2 * WT + FT * (1 + half) + 9 * v + 3 * a + c, slot] = 1.0
                slot = 9 * v + 3 * a + which
                rows[2 * WT + FT * (1 + half) + slot, slot] = 1.0
    for v in range(5):
        rows[2 * WT + 9 * v : 2 * WT + 9 * v + 9, 27 * v : 27 * v + 9] = np.eye(9)
    return rows


def nn(a, b):
    return lax.dot_general(a, b, (((1,), (0,)), ((), ())), preferred_element_type=F32)


def nt(a, b):
    return lax.dot_general(a, b, (((1,), (1,)), ((), ())), preferred_element_type=F32)


def blocks(rows):
    return lax.broadcasted_iota(jnp.int32, (rows, LANES), 1) // R


def by_block(rows, parts):
    block = blocks(rows)
    total = parts[0][1]
    for b, part in parts[1:]:
        total = jnp.where(block == b, part, total)
    return total


def kernel(
    crosses,
    neigh_hbm,
    sel_hbm,
    rhs_hbm,
    init_hbm,
    inv_hbm,
    cpl_hbm,
    out_hbm,
    neigh,
    sel,
    init_v,
    rhs_v,
    out_v,
    inv_n,
    cpl_n,
    turn_v,
    inv_v,
    stack_v,
    d_v,
    rows_v,
    w_v,
    x_v,
    v_v,
    t_v,
    us_v,
    q_v,
    face_v,
    col_v,
    u_v,
    w_face_v,
    l1_v,
    l2_v,
    l3_v,
    li_v,
    e_v,
    mm_v,
    ext_l0,
    ext_l1,
    ext_r0,
    ext_r1,
    up_s,
    up_r,
    a_s,
    a_r,
    m_s,
    m_r,
    load_sem,
    plane_sem,
    out_sem,
    halo_s,
    halo_r,
    upsem,
    a_ss,
    a_rs,
    m_ss,
    m_rs,
):
    ext_l, ext_r = (ext_l0, ext_l1), (ext_r0, ext_r1)
    s = lax.axis_index("sweep")
    k = lax.axis_index("cross")
    right = lax.rem(k + 1, crosses)
    left = lax.rem(k + crosses - 1, crosses)

    load_init = pltpu.make_async_copy(init_hbm, init_v, load_sem.at[0])
    load_rhs = pltpu.make_async_copy(rhs_hbm, rhs_v, load_sem.at[1])

    def inv_load(p):
        return pltpu.make_async_copy(inv_hbm.at[p], inv_n.at[p], plane_sem.at[0, p])

    def cpl_load(p):
        return pltpu.make_async_copy(cpl_hbm.at[p], cpl_n.at[p], plane_sem.at[1, p])

    load_sel = pltpu.make_async_copy(sel_hbm, sel, load_sem.at[2])
    load_neigh = pltpu.make_async_copy(neigh_hbm, neigh, load_sem.at[3])
    load_sel.start()
    load_init.start()
    for p in range(NP):
        inv_load(p).start()
        cpl_load(p).start()
    load_rhs.start()
    load_neigh.start()

    barrier = pltpu.get_barrier_semaphore()
    for other in (left, right):
        pl.semaphore_signal(barrier, inc=1, device_id={"cross": other}, device_id_type=MESH)
    for step in (1, 2, 3):
        pl.semaphore_signal(
            barrier, inc=1, device_id={"sweep": lax.rem(s + step, 4)}, device_id_type=MESH
        )

    def halo(sweep, part):
        def copy(ext, direction, first, to, other):
            return pltpu.make_async_remote_copy(
                ext.at[pl.ds(first + CHUNK * part, CHUNK)],
                ext.at[pl.ds(to + CHUNK * part, CHUNK)],
                halo_s.at[sweep, direction, part],
                halo_r.at[sweep, direction, part],
                device_id={"cross": other},
                device_id_type=MESH,
            )

        return (
            copy(ext_l[sweep], 0, CC, 0, right),
            copy(ext_r[sweep], 1, 0, CC, left),
        )

    up_copy = pltpu.make_async_remote_copy(
        up_s,
        up_r,
        upsem.at[0],
        upsem.at[1],
        device_id={"sweep": lax.rem(s + 3, 4)},
        device_id_type=MESH,
    )

    load_sel.wait()
    load_init.wait()
    up_s[...] = nt(sel[2 * WT : 2 * WT + FT], init_v[0].reshape(CC * R, NU)).astype(BF16)
    for c in range(CC):
        picked = nt(sel[0 : 2 * WT + FT, 0:NU], init_v[:, c].reshape(LANES, NU))
        ext_l[0][CC + c] = picked[0:WT].astype(BF16)
        ext_r[0][c] = picked[WT : 2 * WT].astype(BF16)
        us_v[c] = pltpu.roll(picked[2 * WT : 2 * WT + FT], LANES - R, 1)
        if c == CHUNK - 1:
            pl.semaphore_wait(barrier, 5)
        if c % CHUNK == CHUNK - 1:
            for copy in halo(0, c // CHUNK):
                copy.start()

    @pl.when(s > 0)
    def _():
        up_copy.start()

    def a_copy(sweep, step):
        to = lax.rem(s + step, 4) if sweep == 0 else lax.rem(s + 4 - step, 4)
        return pltpu.make_async_remote_copy(
            a_s.at[sweep],
            a_r.at[sweep, step - 1],
            a_ss.at[sweep, step - 1],
            a_rs.at[sweep, step - 1],
            device_id={"sweep": to},
            device_id_type=MESH,
        )

    def m_copy(sweep, step):
        to = lax.rem(s + step, 4) if sweep == 0 else lax.rem(s + 4 - step, 4)
        return pltpu.make_async_remote_copy(
            m_s.at[sweep],
            m_r.at[sweep, step - 1],
            m_ss.at[sweep, step - 1],
            m_rs.at[sweep, step - 1],
            device_id={"sweep": to},
            device_id_type=MESH,
        )

    def a_sends(sweep, step):
        return s + step < 4 if sweep == 0 else s >= step

    def a_takes(sweep, step):
        return s >= step if sweep == 0 else s + step < 4

    def m_sends(sweep, step):
        if sweep == 0:
            return jnp.logical_and(s >= 1, s + step < 4)
        return jnp.logical_and(s <= 2, s >= step)

    def m_takes(sweep, step):
        return s >= step + 1 if sweep == 0 else s + step <= 2

    @pl.when(s == 3)
    def _():
        up_r[...] = jnp.zeros_like(up_r)

    for step in (1, 2, 3):

        @pl.when(s < step)
        def _():
            a_r[0, step - 1] = jnp.zeros((FT, CC * R), BF16)

        @pl.when(s + step > 3)
        def _():
            a_r[1, step - 1] = jnp.zeros((FT, CC * R), BF16)

    for step in (1, 2):

        @pl.when(s < step + 1)
        def _():
            m_r[0, step - 1] = jnp.zeros((CC, FT, FT), BF16)

        @pl.when(s + step > 2)
        def _():
            m_r[1, step - 1] = jnp.zeros((CC, FT, FT), BF16)

    inv_v[:, :, NU - 7 : NUP] = jnp.zeros((CC, NP, NUP - NU + 7, NU), BF16)
    for place in list(range(len(STACK))) + [LOWER // FT]:
        top = LOWER if place == LOWER // FT else FT * place
        stack_v[:, :, top + 32 : top + FT] = jnp.zeros((CC, NP, 16, NU), BF16)
    stack_v[:, :, NSTACK:LOWER] = jnp.zeros((CC, NP, LOWER - NSTACK, NU), BF16)
    q_v[...] = jnp.zeros_like(q_v)
    for rows in (u_v, w_face_v):
        rows[:, 40:FT] = jnp.zeros((CC, FT - 40, LANES), F32)

    def turn(slot, block, count, to, p, first):
        flat = block.astype(F32).reshape(CC * count, NU)
        turn_v[0, slot, 0 : CC * count] = flat[:, 0:128]
        turn_v[1, slot, 0 : CC * count, 0 : NU - 128] = flat[:, 128:NU]
        for c in range(CC):
            rows = pl.ds(c, count, stride=CC)
            to[c, p, first : first + count, 0:128] = turn_v[0, slot, rows].astype(BF16)
            to[c, p, first : first + count, 128:NU] = turn_v[1, slot, rows][
                :, 0 : NU - 128
            ].astype(BF16)

    def products(p, carry):
        inv_load(p).wait()
        cpl_load(p).wait()
        slot = 0
        for first in range(0, NU, 16):
            count = min(16, NU - first)
            turn(slot, inv_n[p, first : first + count], count, inv_v, p, first)
            slot += 1
        for top, face in [(FT * place, face) for place, face in enumerate(STACK)] + [(LOWER, 0)]:
            for first in range(0, NT, 16):
                count = min(16, NT - first)
                block = cpl_n[p, face, first : first + count]
                turn(slot, block, count, stack_v, p, top + first)
                slot += 1
        for c in range(CC):
            d = nt(inv_v[c, p], stack_v[c, p])
            d_v[c, p] = d.astype(BF16)
            rows_v[c] = d[:, LOWER : LOWER + FT]
            for var in range(5):
                to = slice(9 * var, 9 * var + 9)
                q_v[c, p, to] = rows_v[c, 27 * var + 18 : 27 * var + 27]
        return carry

    lax.fori_loop(0, NP, products, 0)
    load_rhs.wait()

    def by_plane(rows, stacked):
        return by_block(rows, [(p, stacked[rows * p : rows * p + rows]) for p in range(NP)])

    for c in range(CC):
        rhs = rhs_v[:, c].reshape(LANES, NU)
        w_v[c] = by_plane(NUP, nt(inv_v[c].reshape(NP * NUP, NU), rhs))

    def order_of(sweep):
        return list(range(NP)) if sweep == 0 else list(range(NP - 1, -1, -1))

    def d_in(sweep, c):
        low = LOWER if sweep == 0 else 0
        return d_v[c, :, :, low : low + FT]

    def sections(sweep):
        order = order_of(sweep)
        if sweep == 0:
            n = [[(-q_v[c, p]).astype(BF16) for p in order] for c in range(CC)]
        else:
            n = [[-face_v[c, p, :, 0:FT] for p in order] for c in range(CC)]
        two = [
            [nn(n[c][o], n[c][o - 1]).astype(BF16) for o in (1, 2, 3)] for c in range(CC)
        ]
        for c in range(CC):
            for o in (1, 2, 3):
                l1_v[sweep, c, FT * (o - 1) : FT * o] = n[c][o]
            for o in (2, 3):
                l2_v[sweep, c, FT * (o - 2) : FT * (o - 1)] = two[c][o - 1]
            li_v[c, 0] = n[c][0]
            li_v[c, 1] = two[c][0]
            l3_v[sweep, c] = nn(two[c][2], n[c][1]).astype(BF16)
            m_s[sweep, c] = nn(two[c][2], two[c][0]).astype(BF16)
        for step in (1, 2):

            @pl.when(m_sends(sweep, step))
            def _():
                m_copy(sweep, step).start()

    sections(0)

    def fronts_applied(sweep):
        order = order_of(sweep)
        for c in range(CC):
            first = li_v[c, 0]
            fronts = (first, li_v[c, 1], nn(l2_v[sweep, c, 0:FT], first).astype(BF16))
            e_v[sweep, c, order[0]] = d_in(sweep, c)[order[0]]
            for o in (1, 2, 3):
                e_v[sweep, c, order[o]] = nn(d_in(sweep, c)[order[o]], fronts[o - 1]).astype(BF16)

    def gathered(sweep, c, upper):
        low = lax.rem(neigh[2, c] - (k - 1) * CC + 2 * crosses * CC, crosses * CC)
        high = lax.rem(neigh[3, c] - k * CC + crosses * CC, crosses * CC)
        low = jnp.clip(low, 0, 2 * CC - 1)
        high = jnp.clip(high, 0, 2 * CC - 1)
        apart = [sel[2 * WT + FT * half : 2 * WT + FT * half + FT, 0:WT] for half in (1, 2)]
        col_v[c, 0:FT] = upper
        col_v[c, FT : 2 * FT] = nn(apart[0], ext_l[sweep][c]).astype(BF16)
        col_v[c, 2 * FT : 3 * FT] = nn(apart[1], ext_r[sweep][CC + c]).astype(BF16)
        col_v[c, 3 * FT : 4 * FT] = ext_l[sweep][low, 0:FT]
        col_v[c, 4 * FT : 5 * FT] = ext_r[sweep][high, 0:FT]

    def shift_of(sweep, steps):
        return R * steps if sweep == 0 else LANES - R * steps

    def applied_to_column(c):
        d = d_v[c].reshape(NP * NUP, LOWER + FT)[:, 0:NSTACK]
        return by_plane(NUP, nn(d, col_v[c]))

    def local_faces(sweep):
        order = order_of(sweep)
        block = blocks(FT)
        for c in range(CC):
            total = u_v[c]
            for steps, left_v in ((1, l1_v), (2, l2_v), (3, l3_v)):
                moved = pltpu.roll(u_v[c], shift_of(sweep, steps), 1).astype(BF16)
                z = nn(left_v[sweep, c], moved)
                for o in range(steps, NP):
                    part = z[FT * (o - steps) : FT * (o - steps + 1)]
                    total = total + jnp.where(block == order[o], part, 0.0)
            t_v[c] = total
        for g in range(2):
            total = jnp.zeros((FT, LANES), F32)
            for b in range(4):
                total = packed(sweep, b, t_v[4 * g + b], total)
            a_s[sweep, :, LANES * g : LANES * g + LANES] = total.astype(BF16)

    def before_of(sweep, c):
        moved = pltpu.roll(t_v[c], shift_of(sweep, 1), 1)
        return jnp.where(blocks(FT) == order_of(sweep)[0], 0.0, moved).astype(BF16)

    def packed(sweep, b, now, total):
        last = 3 if sweep == 0 else 0
        turned_in = now if b == last else pltpu.roll(now, (R * (b - last)) % LANES, 1)
        return jnp.where(blocks(FT) == b, turned_in, total)

    def spread(b, group):
        one = jnp.where(blocks(FT) == b, group, 0.0)
        one = one + pltpu.roll(one, R, 1)
        return one + pltpu.roll(one, 2 * R, 1)

    def send_ends(sweep):
        for step in (1, 2, 3):

            @pl.when(a_sends(sweep, step))
            def _():
                a_copy(sweep, step).start()

    def take_operators(sweep):
        for step in (1, 2):

            @pl.when(m_takes(sweep, step))
            def _():
                m_copy(sweep, step).wait_recv()

        for c in range(CC):
            mm_v[c] = nn(m_r[sweep, 0, c], m_r[sweep, 1, c]).astype(BF16)

    def take_ends(sweep):
        for step in (1, 2, 3):

            @pl.when(a_takes(sweep, step))
            def _():
                a_copy(sweep, step).wait_recv()

    def incoming(sweep, g):
        lanes = slice(LANES * g, LANES * g + LANES)
        parts = []
        for b in range(4):
            c = 4 * g + b
            one = nn(m_r[sweep, 0, c], a_r[sweep, 1, :, lanes])
            parts.append((b, one + nn(mm_v[c], a_r[sweep, 2, :, lanes])))
        return a_r[sweep, 0, :, lanes].astype(F32) + by_block(FT, parts)

    def corrected(sweep, c, b, entering):
        t = spread(b, entering).astype(BF16)
        return v_v[c] - by_plane(NUP, nn(e_v[sweep, c].reshape(NP * NUP, FT), t))

    load_neigh.wait()
    for part in range(CC // CHUNK):
        for copy in halo(0, part):
            copy.wait_recv()

    @pl.when(s < 3)
    def _():
        up_copy.wait_recv()

    for c in range(CC):
        g, b = c // 4, c % 4
        edge = up_r[:, LANES * g : LANES * g + LANES].astype(F32)
        edge = pltpu.roll(edge, (R * (3 - b)) % LANES, 1) if b != 3 else edge
        gathered(0, c, jnp.where(blocks(FT) == 3, edge, us_v[c]).astype(BF16))
    for c in range(CC):
        x = applied_to_column(c)
        x_v[c] = x
        v_v[c] = w_v[c] - x
        for var in range(5):
            u_v[c, 9 * var : 9 * var + 9] = v_v[c, 27 * var + 18 : 27 * var + 27]
    local_faces(0)
    send_ends(0)
    fronts_applied(0)
    for c in range(CC):
        y = nn(d_in(0, c).reshape(NP * NUP, FT), before_of(0, c))
        v_v[c] = v_v[c] - by_plane(NUP, y)
    take_operators(0)
    take_ends(0)
    for g in range(2):
        entering = incoming(0, g)
        for b in range(4):
            c = 4 * g + b
            middle = corrected(0, c, b, entering)
            picked = nn(sel[0 : 2 * WT, 0:NU], middle[0:NU].astype(BF16)).astype(BF16)
            ext_l[1][CC + c] = picked[0:WT]
            ext_r[1][c] = picked[WT : 2 * WT]
            if c % CHUNK == CHUNK - 1:
                for copy in halo(1, c // CHUNK):
                    copy.start()
            w_v[c] = middle + x_v[c]
    for c in range(CC):
        for p in range(NP):
            face_v[c, p] = nn(sel[2 * WT : 2 * WT + FT], d_v[c, p, 0:NU, 0:NSTACK]).astype(BF16)
        for var in range(5):
            w_face_v[c, 9 * var : 9 * var + 9] = w_v[c, 27 * var : 27 * var + 9]
    sections(1)
    fronts_applied(1)

    for part in range(CC // CHUNK):
        for copy in halo(1, part):
            copy.wait_recv()
    for c in range(CC):
        gathered(1, c, jnp.zeros((FT, LANES), BF16))
    for c in range(CC):
        faces = face_v[c].reshape(NP * FT, NSTACK)
        u_v[c] = w_face_v[c] - by_plane(FT, nn(faces, col_v[c]))
    local_faces(1)
    send_ends(1)
    for c in range(CC):
        col_v[c, 0:FT] = before_of(1, c)
    for c in range(CC):
        v_v[c] = w_v[c] - applied_to_column(c)
    take_operators(1)
    take_ends(1)

    def out_store(c):
        return pltpu.make_async_copy(out_v.at[:, c], out_hbm.at[:, c], out_sem.at[c])

    same = (
        lax.broadcasted_iota(jnp.int32, (LANES, LANES), 0)
        == lax.broadcasted_iota(jnp.int32, (LANES, LANES), 1)
    ).astype(BF16)
    for g in range(2):
        entering = incoming(1, g)
        for b in range(4):
            c = 4 * g + b
            result = corrected(1, c, b, entering)[0:NU].astype(BF16)
            out_v[:, c] = nt(same, result).astype(BF16).reshape(NP, R, NU)
            out_store(c).start()
    for c in range(CC):
        out_store(c).wait()

    for sweep in (0, 1):
        for part in range(CC // CHUNK):
            for copy in halo(sweep, part):
                copy.wait_send()
        for step in (1, 2, 3):

            @pl.when(a_sends(sweep, step))
            def _():
                a_copy(sweep, step).wait_send()

        for step in (1, 2):

            @pl.when(m_sends(sweep, step))
            def _():
                m_copy(sweep, step).wait_send()

    @pl.when(s > 0)
    def _():
        up_copy.wait_send()


def local(crosses, right_sides, initial, inverse_blocks, couplings, neighbours):
    hbm = pl.BlockSpec(memory_space=pltpu.HBM)
    vmem = pltpu.VMEM
    dma = pltpu.SemaphoreType.DMA
    return pl.pallas_call(
        functools.partial(kernel, crosses),
        out_shape=jax.ShapeDtypeStruct(right_sides.shape, BF16),
        in_specs=[
            hbm,
            hbm,
            hbm,
            hbm,
            hbm,
            hbm,
        ],
        out_specs=pl.BlockSpec(memory_space=pl.ANY),
        scratch_shapes=[
            pltpu.SMEM((4, CC), jnp.int32),
            vmem((2 * WT + 3 * FT, NU), BF16),
            vmem((NP, CC, R, NU), BF16),
            vmem((NP, CC, R, NU), BF16),
            vmem((NP, CC, R, NU), BF16),
            vmem((NP, NU, CC, NU), BF16),
            vmem((NP, 6, NT, CC, NU), BF16),
            vmem((2, 27, 16 * CC, 128), F32),
            vmem((CC, NP, NUP, NU), BF16),
            vmem((CC, NP, LOWER + FT, NU), BF16),
            vmem((CC, NP, NUP, LOWER + FT), BF16),
            vmem((CC, NUP, FT), F32),
            vmem((CC, NUP, LANES), F32),
            vmem((CC, NUP, LANES), F32),
            vmem((CC, NUP, LANES), F32),
            vmem((CC, FT, LANES), F32),
            vmem((CC, FT, LANES), F32),
            vmem((CC, NP, FT, FT), F32),
            vmem((CC, NP, FT, NSTACK), BF16),
            vmem((CC, NSTACK, LANES), BF16),
            vmem((CC, FT, LANES), F32),
            vmem((CC, FT, LANES), F32),
            vmem((2, CC, 3 * FT, FT), BF16),
            vmem((2, CC, 2 * FT, FT), BF16),
            vmem((2, CC, FT, FT), BF16),
            vmem((CC, 2, FT, FT), BF16),
            vmem((2, CC, NP, NUP, FT), BF16),
            vmem((CC, FT, FT), BF16),
            vmem((2 * CC, WT, LANES), BF16),
            vmem((2 * CC, WT, LANES), BF16),
            vmem((2 * CC, WT, LANES), BF16),
            vmem((2 * CC, WT, LANES), BF16),
            vmem((FT, CC * R), BF16),
            vmem((FT, CC * R), BF16),
            vmem((2, FT, CC * R), BF16),
            vmem((2, 3, FT, CC * R), BF16),
            vmem((2, CC, FT, FT), BF16),
            vmem((2, 2, CC, FT, FT), BF16),
            dma((4,)),
            dma((2, NP)),
            dma((CC,)),
            dma((2, 2, CC // CHUNK)),
            dma((2, 2, CC // CHUNK)),
            dma((2,)),
            dma((2, 3)),
            dma((2, 3)),
            dma((2, 2)),
            dma((2, 2)),
        ],
        compiler_params=pltpu.CompilerParams(
            collective_id=0, has_side_effects=True, vmem_limit_bytes=56 * 1024 * 1024
        ),
        name="sweeps",
    )(
        neighbours.T,
        jnp.asarray(selector(), BF16),
        right_sides,
        initial,
        inverse_blocks.transpose(0, 2, 1, 3),
        couplings.transpose(0, 2, 3, 1, 4),
    )


def solution(mesh):
    return jax.shard_map(
        functools.partial(local, mesh.shape["cross"]),
        mesh=mesh,
        in_specs=(
            P("sweep", "cross", None, None),
            P("sweep", "cross", None, None),
            P("sweep", "cross", None, None),
            P("sweep", "cross", None, None, None),
            P("cross", None),
        ),
        out_specs=P("sweep", "cross", None, None),
        check_vma=False,
    )
```

```python
import functools

import jax
import jax.numpy as jnp
import numpy as np
from jax import lax
from jax.experimental import pallas as pl
from jax.experimental.pallas import tpu as pltpu
from jax.sharding import PartitionSpec as P

MESH = pl.DeviceIdType.MESH
NU, NT, R, CC, NP = 135, 45, 32, 8, 4
FT = 48
LANES = NP * R
NUP = 144
F32, BF16 = jnp.float32, jnp.bfloat16
WT = 80
STACK = (1, 2, 3, 4, 5)
NSTACK = len(STACK) * FT
LOWER = 256
CHUNK = 2


def selector():
    rows = np.zeros((2 * WT + 3 * FT, NU), np.float32)
    for half, which in enumerate((2, 0)):
        others = [node for node in range(3) if node != which]
        for v in range(5):
            for a in range(3):
                for b in range(3):
                    rows[half * WT + 9 * v + 3 * a + b, 27 * v + 9 * a + 3 * b + which] = 1.0
                for place, c in enumerate(others):
                    slot = NT + 6 * v + 2 * a + place
                    rows[half * WT + slot, 27 * v + 9 * a + 3 * which + c] = 1.0
                    rows[2 * WT + FT * (1 + half) + 9 * v + 3 * a + c, slot] = 1.0
                slot = 9 * v + 3 * a + which
                rows[2 * WT + FT * (1 + half) + slot, slot] = 1.0
    for v in range(5):
        rows[2 * WT + 9 * v : 2 * WT + 9 * v + 9, 27 * v : 27 * v + 9] = np.eye(9)
    return rows


def nn(a, b):
    return lax.dot_general(a, b, (((1,), (0,)), ((), ())), preferred_element_type=F32)


def nt(a, b):
    return lax.dot_general(a, b, (((1,), (1,)), ((), ())), preferred_element_type=F32)


def blocks(rows):
    return lax.broadcasted_iota(jnp.int32, (rows, LANES), 1) // R


def by_block(rows, parts):
    block = blocks(rows)
    total = parts[0][1]
    for b, part in parts[1:]:
        total = jnp.where(block == b, part, total)
    return total


def kernel(
    crosses,
    neigh_hbm,
    sel_hbm,
    rhs_hbm,
    init_hbm,
    inv_hbm,
    cpl_hbm,
    out_hbm,
    neigh,
    sel,
    init_v,
    rhs_v,
    out_v,
    inv_n,
    cpl_n,
    turn_v,
    inv_v,
    stack_v,
    d_v,
    rows_v,
    w_v,
    x_v,
    v_v,
    t_v,
    us_v,
    q_v,
    face_v,
    col_v,
    u_v,
    w_face_v,
    l1_v,
    l2_v,
    l3_v,
    li_v,
    e_v,
    mm_v,
    ext_l0,
    ext_l1,
    ext_r0,
    ext_r1,
    up_s,
    up_r,
    a_s,
    a_r,
    m_s,
    m_r,
    load_sem,
    plane_sem,
    out_sem,
    halo_s,
    halo_r,
    upsem,
    a_ss,
    a_rs,
    m_ss,
    m_rs,
):
    ext_l, ext_r = (ext_l0, ext_l1), (ext_r0, ext_r1)
    s = lax.axis_index("sweep")
    k = lax.axis_index("cross")
    right = lax.rem(k + 1, crosses)
    left = lax.rem(k + crosses - 1, crosses)

    load_init = pltpu.make_async_copy(init_hbm, init_v, load_sem.at[0])
    load_rhs = pltpu.make_async_copy(rhs_hbm, rhs_v, load_sem.at[1])

    def inv_load(p):
        return pltpu.make_async_copy(inv_hbm.at[p], inv_n.at[p], plane_sem.at[0, p])

    def cpl_load(p):
        return pltpu.make_async_copy(cpl_hbm.at[p], cpl_n.at[p], plane_sem.at[1, p])

    load_sel = pltpu.make_async_copy(sel_hbm, sel, load_sem.at[2])
    load_neigh = pltpu.make_async_copy(neigh_hbm, neigh, load_sem.at[3])
    load_sel.start()
    load_init.start()
    for p in range(NP):
        inv_load(p).start()
        cpl_load(p).start()
    load_rhs.start()
    load_neigh.start()

    barrier = pltpu.get_barrier_semaphore()
    for other in (left, right):
        pl.semaphore_signal(barrier, inc=1, device_id={"cross": other}, device_id_type=MESH)
    for step in (1, 2, 3):
        pl.semaphore_signal(
            barrier, inc=1, device_id={"sweep": lax.rem(s + step, 4)}, device_id_type=MESH
        )

    def halo(sweep, part):
        def copy(ext, direction, first, to, other):
            return pltpu.make_async_remote_copy(
                ext.at[pl.ds(first + CHUNK * part, CHUNK)],
                ext.at[pl.ds(to + CHUNK * part, CHUNK)],
                halo_s.at[sweep, direction, part],
                halo_r.at[sweep, direction, part],
                device_id={"cross": other},
                device_id_type=MESH,
            )

        return (
            copy(ext_l[sweep], 0, CC, 0, right),
            copy(ext_r[sweep], 1, 0, CC, left),
        )

    up_copy = pltpu.make_async_remote_copy(
        up_s,
        up_r,
        upsem.at[0],
        upsem.at[1],
        device_id={"sweep": lax.rem(s + 3, 4)},
        device_id_type=MESH,
    )

    inv_v[:, :, NU - 7 : NUP] = jnp.zeros((CC, NP, NUP - NU + 7, NU), BF16)
    for place in list(range(len(STACK))) + [LOWER // FT]:
        top = LOWER if place == LOWER // FT else FT * place
        stack_v[:, :, top + 32 : top + FT] = jnp.zeros((CC, NP, 16, NU), BF16)
    stack_v[:, :, NSTACK:LOWER] = jnp.zeros((CC, NP, LOWER - NSTACK, NU), BF16)
    q_v[...] = jnp.zeros_like(q_v)
    for rows in (u_v, w_face_v):
        rows[:, 40:FT] = jnp.zeros((CC, FT - 40, LANES), F32)

    load_sel.wait()
    load_init.wait()
    up_s[...] = nt(sel[2 * WT : 2 * WT + FT], init_v[0].reshape(CC * R, NU)).astype(BF16)
    for c in range(CC):
        picked = nt(sel[0 : 2 * WT + FT, 0:NU], init_v[:, c].reshape(LANES, NU))
        ext_l[0][CC + c] = picked[0:WT].astype(BF16)
        ext_r[0][c] = picked[WT : 2 * WT].astype(BF16)
        us_v[c] = pltpu.roll(picked[2 * WT : 2 * WT + FT], LANES - R, 1)
        if c == CHUNK - 1:
            pl.semaphore_wait(barrier, 5)
        if c % CHUNK == CHUNK - 1:
            for copy in halo(0, c // CHUNK):
                copy.start()

    @pl.when(s > 0)
    def _():
        up_copy.start()

    def a_copy(sweep, step):
        to = lax.rem(s + step, 4) if sweep == 0 else lax.rem(s + 4 - step, 4)
        return pltpu.make_async_remote_copy(
            a_s.at[sweep],
            a_r.at[sweep, step - 1],
            a_ss.at[sweep, step - 1],
            a_rs.at[sweep, step - 1],
            device_id={"sweep": to},
            device_id_type=MESH,
        )

    def m_copy(sweep, step):
        to = lax.rem(s + step, 4) if sweep == 0 else lax.rem(s + 4 - step, 4)
        return pltpu.make_async_remote_copy(
            m_s.at[sweep],
            m_r.at[sweep, step - 1],
            m_ss.at[sweep, step - 1],
            m_rs.at[sweep, step - 1],
            device_id={"sweep": to},
            device_id_type=MESH,
        )

    def a_sends(sweep, step):
        return s + step < 4 if sweep == 0 else s >= step

    def a_takes(sweep, step):
        return s >= step if sweep == 0 else s + step < 4

    def m_sends(sweep, step):
        if sweep == 0:
            return jnp.logical_and(s >= 1, s + step < 4)
        return jnp.logical_and(s <= 2, s >= step)

    def m_takes(sweep, step):
        return s >= step + 1 if sweep == 0 else s + step <= 2

    @pl.when(s == 3)
    def _():
        up_r[...] = jnp.zeros_like(up_r)

    for step in (1, 2, 3):

        @pl.when(s < step)
        def _():
            a_r[0, step - 1] = jnp.zeros((FT, CC * R), BF16)

        @pl.when(s + step > 3)
        def _():
            a_r[1, step - 1] = jnp.zeros((FT, CC * R), BF16)

    for step in (1, 2):

        @pl.when(s < step + 1)
        def _():
            m_r[0, step - 1] = jnp.zeros((CC, FT, FT), BF16)

        @pl.when(s + step > 2)
        def _():
            m_r[1, step - 1] = jnp.zeros((CC, FT, FT), BF16)

    def turn(slot, block, count, to, p, first):
        flat = block.astype(F32).reshape(CC * count, NU)
        turn_v[0, slot, 0 : CC * count] = flat[:, 0:128]
        turn_v[1, slot, 0 : CC * count, 0 : NU - 128] = flat[:, 128:NU]
        for c in range(CC):
            rows = pl.ds(c, count, stride=CC)
            to[c, p, first : first + count, 0:128] = turn_v[0, slot, rows].astype(BF16)
            to[c, p, first : first + count, 128:NU] = turn_v[1, slot, rows][
                :, 0 : NU - 128
            ].astype(BF16)

    def products(p, carry):
        inv_load(p).wait()
        cpl_load(p).wait()
        slot = 0
        for first in range(0, NU, 16):
            count = min(16, NU - first)
            turn(slot, inv_n[p, first : first + count], count, inv_v, p, first)
            slot += 1
        for top, face in [(FT * place, face) for place, face in enumerate(STACK)] + [(LOWER, 0)]:
            for first in range(0, NT, 16):
                count = min(16, NT - first)
                block = cpl_n[p, face, first : first + count]
                turn(slot, block, count, stack_v, p, top + first)
                slot += 1
        for c in range(CC):
            d = nt(inv_v[c, p], stack_v[c, p])
            d_v[c, p] = d.astype(BF16)
            rows_v[c] = d[:, LOWER : LOWER + FT]
            for var in range(5):
                to = slice(9 * var, 9 * var + 9)
                q_v[c, p, to] = rows_v[c, 27 * var + 18 : 27 * var + 27]
        return carry

    lax.fori_loop(0, NP, products, 0)
    load_rhs.wait()

    def by_plane(rows, stacked):
        return by_block(rows, [(p, stacked[rows * p : rows * p + rows]) for p in range(NP)])

    for c in range(CC):
        rhs = rhs_v[:, c].reshape(LANES, NU)
        w_v[c] = by_plane(NUP, nt(inv_v[c].reshape(NP * NUP, NU), rhs))

    def order_of(sweep):
        return list(range(NP)) if sweep == 0 else list(range(NP - 1, -1, -1))

    def d_in(sweep, c):
        low = LOWER if sweep == 0 else 0
        return d_v[c, :, :, low : low + FT]

    def sections(sweep):
        order = order_of(sweep)
        if sweep == 0:
            n = [[(-q_v[c, p]).astype(BF16) for p in order] for c in range(CC)]
        else:
            n = [[-face_v[c, p, :, 0:FT] for p in order] for c in range(CC)]
        two = [
            [nn(n[c][o], n[c][o - 1]).astype(BF16) for o in (1, 2, 3)] for c in range(CC)
        ]
        for c in range(CC):
            for o in (1, 2, 3):
                l1_v[sweep, c, FT * (o - 1) : FT * o] = n[c][o]
            for o in (2, 3):
                l2_v[sweep, c, FT * (o - 2) : FT * (o - 1)] = two[c][o - 1]
            li_v[c, 0] = n[c][0]
            li_v[c, 1] = two[c][0]
            l3_v[sweep, c] = nn(two[c][2], n[c][1]).astype(BF16)
            m_s[sweep, c] = nn(two[c][2], two[c][0]).astype(BF16)
        for step in (1, 2):

            @pl.when(m_sends(sweep, step))
            def _():
                m_copy(sweep, step).start()

    sections(0)

    def fronts_applied(sweep):
        order = order_of(sweep)
        for c in range(CC):
            first = li_v[c, 0]
            fronts = (first, li_v[c, 1], nn(l2_v[sweep, c, 0:FT], first).astype(BF16))
            e_v[sweep, c, order[0]] = d_in(sweep, c)[order[0]]
            for o in (1, 2, 3):
                e_v[sweep, c, order[o]] = nn(d_in(sweep, c)[order[o]], fronts[o - 1]).astype(BF16)

    def gathered(sweep, c, upper):
        low = lax.rem(neigh[2, c] - (k - 1) * CC + 2 * crosses * CC, crosses * CC)
        high = lax.rem(neigh[3, c] - k * CC + crosses * CC, crosses * CC)
        low = jnp.clip(low, 0, 2 * CC - 1)
        high = jnp.clip(high, 0, 2 * CC - 1)
        apart = [sel[2 * WT + FT * half : 2 * WT + FT * half + FT, 0:WT] for half in (1, 2)]
        col_v[c, 0:FT] = upper
        col_v[c, FT : 2 * FT] = nn(apart[0], ext_l[sweep][c]).astype(BF16)
        col_v[c, 2 * FT : 3 * FT] = nn(apart[1], ext_r[sweep][CC + c]).astype(BF16)
        col_v[c, 3 * FT : 4 * FT] = ext_l[sweep][low, 0:FT]
        col_v[c, 4 * FT : 5 * FT] = ext_r[sweep][high, 0:FT]

    def shift_of(sweep, steps):
        return R * steps if sweep == 0 else LANES - R * steps

    def applied_to_column(c):
        d = d_v[c].reshape(NP * NUP, LOWER + FT)[:, 0:NSTACK]
        return by_plane(NUP, nn(d, col_v[c]))

    def local_faces(sweep):
        order = order_of(sweep)
        block = blocks(FT)
        for c in range(CC):
            total = u_v[c]
            for steps, left_v in ((1, l1_v), (2, l2_v), (3, l3_v)):
                moved = pltpu.roll(u_v[c], shift_of(sweep, steps), 1).astype(BF16)
                z = nn(left_v[sweep, c], moved)
                for o in range(steps, NP):
                    part = z[FT * (o - steps) : FT * (o - steps + 1)]
                    total = total + jnp.where(block == order[o], part, 0.0)
            t_v[c] = total
        for g in range(2):
            total = jnp.zeros((FT, LANES), F32)
            for b in range(4):
                total = packed(sweep, b, t_v[4 * g + b], total)
            a_s[sweep, :, LANES * g : LANES * g + LANES] = total.astype(BF16)

    def before_of(sweep, c):
        moved = pltpu.roll(t_v[c], shift_of(sweep, 1), 1)
        return jnp.where(blocks(FT) == order_of(sweep)[0], 0.0, moved).astype(BF16)

    def packed(sweep, b, now, total):
        last = 3 if sweep == 0 else 0
        turned_in = now if b == last else pltpu.roll(now, (R * (b - last)) % LANES, 1)
        return jnp.where(blocks(FT) == b, turned_in, total)

    def spread(b, group):
        one = jnp.where(blocks(FT) == b, group, 0.0)
        one = one + pltpu.roll(one, R, 1)
        return one + pltpu.roll(one, 2 * R, 1)

    def send_ends(sweep):
        for step in (1, 2, 3):

            @pl.when(a_sends(sweep, step))
            def _():
                a_copy(sweep, step).start()

    def take_operators(sweep):
        for step in (1, 2):

            @pl.when(m_takes(sweep, step))
            def _():
                m_copy(sweep, step).wait_recv()

        for c in range(CC):
            mm_v[c] = nn(m_r[sweep, 0, c], m_r[sweep, 1, c]).astype(BF16)

    def take_ends(sweep):
        for step in (1, 2, 3):

            @pl.when(a_takes(sweep, step))
            def _():
                a_copy(sweep, step).wait_recv()

    def incoming(sweep, g):
        lanes = slice(LANES * g, LANES * g + LANES)
        parts = []
        for b in range(4):
            c = 4 * g + b
            one = nn(m_r[sweep, 0, c], a_r[sweep, 1, :, lanes])
            parts.append((b, one + nn(mm_v[c], a_r[sweep, 2, :, lanes])))
        return a_r[sweep, 0, :, lanes].astype(F32) + by_block(FT, parts)

    def corrected(sweep, c, b, entering):
        t = spread(b, entering).astype(BF16)
        return v_v[c] - by_plane(NUP, nn(e_v[sweep, c].reshape(NP * NUP, FT), t))

    load_neigh.wait()
    for part in range(CC // CHUNK):
        for copy in halo(0, part):
            copy.wait_recv()

    @pl.when(s < 3)
    def _():
        up_copy.wait_recv()

    for c in range(CC):
        g, b = c // 4, c % 4
        edge = up_r[:, LANES * g : LANES * g + LANES].astype(F32)
        edge = pltpu.roll(edge, (R * (3 - b)) % LANES, 1) if b != 3 else edge
        gathered(0, c, jnp.where(blocks(FT) == 3, edge, us_v[c]).astype(BF16))
    for c in range(CC):
        x = applied_to_column(c)
        x_v[c] = x
        v_v[c] = w_v[c] - x
        for var in range(5):
            u_v[c, 9 * var : 9 * var + 9] = v_v[c, 27 * var + 18 : 27 * var + 27]
    local_faces(0)
    send_ends(0)
    fronts_applied(0)
    for c in range(CC):
        y = nn(d_in(0, c).reshape(NP * NUP, FT), before_of(0, c))
        v_v[c] = v_v[c] - by_plane(NUP, y)
    take_operators(0)
    take_ends(0)
    for g in range(2):
        entering = incoming(0, g)
        for b in range(4):
            c = 4 * g + b
            middle = corrected(0, c, b, entering)
            picked = nn(sel[0 : 2 * WT, 0:NU], middle[0:NU].astype(BF16)).astype(BF16)
            ext_l[1][CC + c] = picked[0:WT]
            ext_r[1][c] = picked[WT : 2 * WT]
            if c % CHUNK == CHUNK - 1:
                for copy in halo(1, c // CHUNK):
                    copy.start()
            w_v[c] = middle + x_v[c]
    for c in range(CC):
        for p in range(NP):
            face_v[c, p] = nn(sel[2 * WT : 2 * WT + FT], d_v[c, p, 0:NU, 0:NSTACK]).astype(BF16)
        for var in range(5):
            w_face_v[c, 9 * var : 9 * var + 9] = w_v[c, 27 * var : 27 * var + 9]
    sections(1)
    fronts_applied(1)

    for part in range(CC // CHUNK):
        for copy in halo(1, part):
            copy.wait_recv()
    for c in range(CC):
        gathered(1, c, jnp.zeros((FT, LANES), BF16))
    for c in range(CC):
        faces = face_v[c].reshape(NP * FT, NSTACK)
        u_v[c] = w_face_v[c] - by_plane(FT, nn(faces, col_v[c]))
    local_faces(1)
    send_ends(1)
    for c in range(CC):
        col_v[c, 0:FT] = before_of(1, c)
    for c in range(CC):
        v_v[c] = w_v[c] - applied_to_column(c)
    take_operators(1)
    take_ends(1)

    def out_store(c):
        return pltpu.make_async_copy(out_v.at[:, c], out_hbm.at[:, c], out_sem.at[c])

    same = (
        lax.broadcasted_iota(jnp.int32, (LANES, LANES), 0)
        == lax.broadcasted_iota(jnp.int32, (LANES, LANES), 1)
    ).astype(BF16)
    for g in range(2):
        entering = incoming(1, g)
        for b in range(4):
            c = 4 * g + b
            result = corrected(1, c, b, entering)[0:NU].astype(BF16)
            out_v[:, c] = nt(same, result).astype(BF16).reshape(NP, R, NU)
            out_store(c).start()
    for c in range(CC):
        out_store(c).wait()

    for sweep in (0, 1):
        for part in range(CC // CHUNK):
            for copy in halo(sweep, part):
                copy.wait_send()
        for step in (1, 2, 3):

            @pl.when(a_sends(sweep, step))
            def _():
                a_copy(sweep, step).wait_send()

        for step in (1, 2):

            @pl.when(m_sends(sweep, step))
            def _():
                m_copy(sweep, step).wait_send()

    @pl.when(s > 0)
    def _():
        up_copy.wait_send()


def local(crosses, right_sides, initial, inverse_blocks, couplings, neighbours):
    hbm = pl.BlockSpec(memory_space=pltpu.HBM)
    vmem = pltpu.VMEM
    dma = pltpu.SemaphoreType.DMA
    return pl.pallas_call(
        functools.partial(kernel, crosses),
        out_shape=jax.ShapeDtypeStruct(right_sides.shape, BF16),
        in_specs=[
            hbm,
            hbm,
            hbm,
            hbm,
            hbm,
            hbm,
        ],
        out_specs=pl.BlockSpec(memory_space=pl.ANY),
        scratch_shapes=[
            pltpu.SMEM((4, CC), jnp.int32),
            vmem((2 * WT + 3 * FT, NU), BF16),
            vmem((NP, CC, R, NU), BF16),
            vmem((NP, CC, R, NU), BF16),
            vmem((NP, CC, R, NU), BF16),
            vmem((NP, NU, CC, NU), BF16),
            vmem((NP, 6, NT, CC, NU), BF16),
            vmem((2, 27, 16 * CC, 128), F32),
            vmem((CC, NP, NUP, NU), BF16),
            vmem((CC, NP, LOWER + FT, NU), BF16),
            vmem((CC, NP, NUP, LOWER + FT), BF16),
            vmem((CC, NUP, FT), F32),
            vmem((CC, NUP, LANES), F32),
            vmem((CC, NUP, LANES), F32),
            vmem((CC, NUP, LANES), F32),
            vmem((CC, FT, LANES), F32),
            vmem((CC, FT, LANES), F32),
            vmem((CC, NP, FT, FT), F32),
            vmem((CC, NP, FT, NSTACK), BF16),
            vmem((CC, NSTACK, LANES), BF16),
            vmem((CC, FT, LANES), F32),
            vmem((CC, FT, LANES), F32),
            vmem((2, CC, 3 * FT, FT), BF16),
            vmem((2, CC, 2 * FT, FT), BF16),
            vmem((2, CC, FT, FT), BF16),
            vmem((CC, 2, FT, FT), BF16),
            vmem((2, CC, NP, NUP, FT), BF16),
            vmem((CC, FT, FT), BF16),
            vmem((2 * CC, WT, LANES), BF16),
            vmem((2 * CC, WT, LANES), BF16),
            vmem((2 * CC, WT, LANES), BF16),
            vmem((2 * CC, WT, LANES), BF16),
            vmem((FT, CC * R), BF16),
            vmem((FT, CC * R), BF16),
            vmem((2, FT, CC * R), BF16),
            vmem((2, 3, FT, CC * R), BF16),
            vmem((2, CC, FT, FT), BF16),
            vmem((2, 2, CC, FT, FT), BF16),
            dma((4,)),
            dma((2, NP)),
            dma((CC,)),
            dma((2, 2, CC // CHUNK)),
            dma((2, 2, CC // CHUNK)),
            dma((2,)),
            dma((2, 3)),
            dma((2, 3)),
            dma((2, 2)),
            dma((2, 2)),
        ],
        compiler_params=pltpu.CompilerParams(
            collective_id=0, has_side_effects=True, vmem_limit_bytes=56 * 1024 * 1024
        ),
        name="sweeps",
    )(
        neighbours.T,
        jnp.asarray(selector(), BF16),
        right_sides,
        initial,
        inverse_blocks.transpose(0, 2, 1, 3),
        couplings.transpose(0, 2, 3, 1, 4),
    )


def solution(mesh):
    return jax.shard_map(
        functools.partial(local, mesh.shape["cross"]),
        mesh=mesh,
        in_specs=(
            P("sweep", "cross", None, None),
            P("sweep", "cross", None, None),
            P("sweep", "cross", None, None),
            P("sweep", "cross", None, None, None),
            P("cross", None),
        ),
        out_specs=P("sweep", "cross", None, None),
        check_vma=False,
    )
```
